128 devices in a mesh: aux: 8 (over y, core), virt: 16 (over z, x).
Axes of the slice: x: 4, y: 4, z: 4, core: 2. Of those that a mesh axis runs over, the one named last changes fastest.
Arguments:
- integrals: float32 [1024, 6, 2560], P('virt', None, 'aux'), may hold values from -1.25 to 1.25
- metric_root: float32 [2560, 2560], P(None, 'aux'), may hold values from -0.125 to 0.125
- occ_energy: float32 [256], replicated, may hold values from -1.5 to -0.3
- virt_energy: float32 [1024], replicated, may hold values from 0.2 to 3
- batch_index: int32 [6], replicated, may hold values from 0 to 255, as said below
- virt_order: int32 [1024], replicated, may hold values from 0 to 1023, each once
Outputs:
- density: float32 [1024, 6, 2560], P('virt', None, 'aux')
The draws below stay inside these ranges and needn't reach their ends.
Inputs may be any that keep to these rules, and one draw needn't show every extreme that they name: `batch_index`: 6 distinct occupied orbital numbers, among them 0 and 255. `virt_order`: each number appears once.
All inputs are finite; a program needn't handle non-finite values.
Results may differ from the reference program's by a relative error of at most 0.000057.
Values sent between devices are 32-bit elements; how exact they have to be, the bound alone decides.
No kernel may reach another device: no remote copies, remote signals or barrier semaphores. Data moves between devices by JAX's collectives and lax.ppermute only.
A program may use at most 128 MiB of HBM per device.

```python
import jax
import jax.numpy as jnp
from jax import lax

NV = 1024
NAUX = 2560
NOCC_ALL = 256
OB = 6


def draw_batch_index(key, part):
    first_key = jax.random.fold_in(key, 11)
    second_key = jax.random.fold_in(key, 23)
    middle = (jax.random.permutation(first_key, NOCC_ALL - 2)[:OB - 2] + 1).astype(jnp.int32)
    ends = jnp.array([0, NOCC_ALL - 1], dtype=jnp.int32)
    chosen = jnp.concatenate([ends, middle], axis=0)
    return jax.random.permutation(second_key, chosen).astype(jnp.int32)


def steps_of(key, extent, cuts, least, high):
    def one(axis_at, parts):
        heights = jax.random.uniform(jax.random.fold_in(jax.random.fold_in(key, 6), axis_at), (parts,), jnp.float32, least / len(cuts), high / len(cuts))
        return jnp.repeat(jnp.exp(heights), extent[axis_at] // parts).reshape((-1,) + (1,) * (len(extent) - axis_at - 1))

    factor_of = one(*cuts[0])
    for cut in cuts[1:]:
        factor_of = factor_of * one(*cut)
    return factor_of


def scatter_about(rng, dims, width, reach, shards=(), kind=jnp.bfloat16):
    result = jax.random.normal(rng, dims, jnp.float32) * width
    if len(shards) > 0:
        result = steps_of(rng, dims, shards, -0.22, 0.18) * result
    return jnp.clip(result, min=-reach, max=reach).astype(kind)


def setup_inputs(seed: int = 0) -> dict:
    seeds = jax.random.split(jax.random.key(seed), 7)
    integrals = scatter_about(seeds[0], (NV, OB, NAUX), 0.09, 1.25, ((0, 16), (2, 8)), jnp.float32)
    metric_root = scatter_about(seeds[1], (NAUX, NAUX), NAUX ** -0.5, 0.125, ((1, 8),), jnp.float32)
    occ_energy = jnp.clip(jax.random.uniform(seeds[2], (NOCC_ALL,), jnp.float32, -1.5, -0.3), -1.5, -0.3)
    virt_energy = jnp.clip(jax.random.uniform(seeds[3], (NV,), jnp.float32, 0.2, 3.0), 0.2, 3.0)
    batch_index = draw_batch_index(jax.random.fold_in(seeds[6], 71), 0)
    virt_order = jax.random.permutation(seeds[5], NV).astype(jnp.int32)
    return {"integrals": integrals, "metric_root": metric_root, "occ_energy": occ_energy, "virt_energy": virt_energy, "batch_index": batch_index, "virt_order": virt_order}


precise = lax.Precision.HIGHEST
block_size = 64


def pair_density(left_rows, right_rows, row_levels, col_levels, occ_levels):
    row_count = row_levels.shape[0]
    col_count = col_levels.shape[0]
    occ_count = occ_levels.shape[0]
    pair_ints = lax.dot_general(left_rows, right_rows, (((1,), (1,)), ((), ())), precision=precise, preferred_element_type=jnp.float32)
    pair_ints = pair_ints.reshape(row_count, occ_count, col_count, occ_count)
    swapped = pair_ints.transpose(0, 3, 2, 1)
    denominator = occ_levels[None, :, None, None] + occ_levels[None, None, None, :] - row_levels[:, None, None, None] - col_levels[None, None, :, None]
    weighted = ((2.0 * pair_ints - swapped) / denominator).reshape(row_count * occ_count, col_count * occ_count)
    return jnp.dot(weighted, right_rows, precision=precise, preferred_element_type=jnp.float32)


def reference(integrals, metric_root, occ_energy, virt_energy, batch_index, virt_order):
    virt_total, batch_count, aux_total = integrals.shape
    occ_levels = occ_energy[batch_index]
    virt_levels = virt_energy[virt_order]
    flattened = integrals.reshape(virt_total * batch_count, aux_total)
    fitted = lax.dot_general(flattened, metric_root, (((1,), (1,)), ((), ())), precision=precise, preferred_element_type=jnp.float32)

    def block_density(start_row):
        left_rows = lax.dynamic_slice_in_dim(fitted, start_row * batch_count, block_size * batch_count, 0)
        row_levels = lax.dynamic_slice_in_dim(virt_levels, start_row, block_size, 0)
        return pair_density(left_rows, fitted, row_levels, virt_levels, occ_levels)

    block_starts = (jnp.arange(virt_total // block_size) * block_size).astype(jnp.int32)
    blocks = lax.map(block_density, block_starts)
    return blocks.reshape(virt_total, batch_count, aux_total)
```

```python
import jax
import jax.numpy as jnp
from jax import lax
from jax.experimental import pallas as pl
from jax.experimental.pallas import tpu as pltpu
from jax.sharding import PartitionSpec as P


F32 = jnp.float32
BF16 = jnp.bfloat16
OCC = 6
VL = 64
QL = 320
QH = 1280
QT = QH // 128


def plane(dz, dx):
    return [(z * 4 + x, (z + dz) % 4 * 4 + (x + dx) % 4) for z in range(4) for x in range(4)]


def column(place, swap):
    return [(y * 2 + c, place(y) * 2 + (c ^ swap)) for y in range(4) for c in range(2)]


XP, XM, X2 = plane(0, 1), plane(0, -1), plane(0, 2)
ZP, ZM, Z2 = plane(1, 0), plane(-1, 0), plane(2, 0)
YA = column(lambda y: y ^ 1, 0)
YB = column(lambda y: 3 - y, 0)
CORE = column(lambda y: y, 1)


def on_virt(value, pairs):
    return lax.ppermute(value, "virt", pairs)


def on_aux(value, pairs):
    return lax.ppermute(value, "aux", pairs)


def split(value):
    high = value.astype(BF16)
    return high, (value - high.astype(F32)).astype(BF16)


def product(left, right, dims):
    left_high, left_low = left
    right_high, right_low = right

    def one(a, b):
        return lax.dot_general(a, b, (dims, ((), ())), preferred_element_type=F32)

    return one(left_high, right_low) + one(left_low, right_high) + one(left_high, right_high)


def half_turn(value):
    return pltpu.roll(value, 64, 1)


def lanes(rows):
    return lax.broadcasted_iota(jnp.int32, (rows, 128), 1) < 64


def fitted_kernel(places, integrals, metric, sent, kept, right, full):
    core = places[0]
    for y in range(4):
        start = pl.multiple_of(640 * y + 384 * core, 128)
        right[:, 256 * y : 256 * y + 256] = metric[:, pl.ds(start, 256)]
    low = lanes(QL)
    for p in range(2):
        first = metric[:, 1280 * p + 256 : 1280 * p + 384]
        second = metric[:, 1280 * p + 896 : 1280 * p + 1024]
        even = jnp.where(low, first, half_turn(second))
        odd = jnp.where(low, half_turn(first), second)
        right[:, 1024 + 128 * p : 1152 + 128 * p] = jnp.where(core == 0, even, odd)
    left = integrals[...].reshape(OCC * VL, QL)
    value = product(split(left), split(right[...]), ((1,), (0,)))
    full[...] = value.reshape(OCC, 4, 2, 8, QH)
    y_a, y_b, y_far, y_own = places[1], places[2], places[3], places[4]
    for target, half, slot, y in (
        (sent, 0, 0, y_a), (sent, 0, 1, y_far), (sent, 1, 0, y_b), (sent, 1, 1, y_far),
        (kept, 0, 0, y_own), (kept, 0, 1, y_b), (kept, 1, 0, y_own), (kept, 1, 1, y_a),
    ):
        for i in range(OCC):
            for q in range(QT):
                target[half, slot, i, q] = full[i, y, half, :, 128 * q : 128 * q + 128]


def fitted_part(places, integrals, metric, name):
    piece = jax.ShapeDtypeStruct((2, 2, OCC, QT, 8, 128), F32)
    return pl.pallas_call(
        fitted_kernel,
        out_shape=(piece, piece),
        in_specs=[
            pl.BlockSpec(memory_space=pltpu.SMEM),
            pl.BlockSpec(memory_space=pltpu.VMEM),
            pl.BlockSpec(memory_space=pltpu.VMEM),
        ],
        out_specs=(pl.BlockSpec(memory_space=pltpu.VMEM),) * 2,
        scratch_shapes=[pltpu.VMEM((QL, QH), F32), pltpu.VMEM((OCC, 4, 2, 8, QH), F32)],
        name=name,
    )(places, integrals, metric)


def rows_of(refs):
    own, near_a, near_b, far_0, far_1 = refs
    return [(own, (0,)), (own, (1,)), (near_a, (0,)), (near_a, (1,)), (near_b, (0,)), (near_b, (1,)), (far_0, ()), (far_1, ())]


def cols_of(refs):
    blocks = []
    for ref in refs:
        blocks += [(ref, ())] if len(ref.shape) == 4 else [(ref, (k,)) for k in range(ref.shape[0])]
    return blocks


def lay(target, blocks):
    count = len(blocks)
    for k, (ref, at) in enumerate(blocks):
        for i in range(OCC):
            row = (i * count + k) * 8
            for q in range(QT):
                target[row : row + 8, 128 * q : 128 * q + 128] = ref[(*at, i, q)]


def pair_kernel(count, *refs):
    rows, cols = refs[:5], refs[5 : 5 + count]
    result, left, right = refs[5 + count :]
    lay(left, rows_of(rows))
    lay(right, cols_of(cols))
    result[...] = product(split(left[...]), split(right[...]), ((1,), (1,)))


def half_shards(cols):
    return sum(1 if c.ndim == 4 else c.shape[0] for c in cols)


def pair_part(rows, cols, name):
    width = half_shards(cols) * 48

    def kernel(*refs):
        pair_kernel(len(cols), *refs)

    return pl.pallas_call(
        kernel,
        out_shape=jax.ShapeDtypeStruct((OCC * VL, width), F32),
        in_specs=[pl.BlockSpec(memory_space=pltpu.VMEM)] * (5 + len(cols)),
        out_specs=pl.BlockSpec(memory_space=pltpu.VMEM),
        scratch_shapes=[pltpu.VMEM((OCC * VL, QH), F32), pltpu.VMEM((width, QH), F32)],
        name=name,
    )(*rows, *cols)


def amplitudes(pair, row_term, col_term):
    width = pair.shape[1]
    each = width // OCC
    low = lanes(VL)
    pieces = []
    for i in range(OCC):
        swapped = []
        if each == 128:
            for j in range(OCC):
                swapped.append(pair[VL * j : VL * j + VL, 128 * i : 128 * i + 128])
        else:
            at = 128 * (i // 2)
            for t in range(OCC // 2):
                first = pair[2 * t * VL : 2 * t * VL + VL, at : at + 128]
                second = pair[(2 * t + 1) * VL : (2 * t + 2) * VL, at : at + 128]
                if i % 2 == 0:
                    second = half_turn(second)
                else:
                    first = half_turn(first)
                swapped.append(jnp.where(low, first, second))
        direct = pair[VL * i : VL * i + VL, :]
        levels = row_term[VL * i : VL * i + VL, :] + col_term
        pieces.append((2.0 * direct - jnp.concatenate(swapped, axis=1)) / levels)
    return jnp.concatenate(pieces, axis=0)


def density_term(refs, count):
    own, other, row_term, col_term = refs[:4]
    cols = refs[4 : 4 + count]
    right = refs[-1]
    lay(right, cols_of(cols))
    amplitude = amplitudes(own[...] + other[...], row_term[...], col_term[...])
    return product(split(amplitude), split(right[...]), ((1,), (0,)))


def density_part(own, other, row_term, col_term, cols, before, name):
    width = half_shards(cols) * 48
    count = len(cols)

    def kernel(*refs):
        term = density_term((*refs[: 4 + count], refs[-1]), count)
        result = refs[-2]
        if before is None:
            result[...] = term
        else:
            result[...] = refs[4 + count][...] + term

    args = (own, other, row_term, col_term, *cols) + (() if before is None else (before,))
    return pl.pallas_call(
        kernel,
        out_shape=jax.ShapeDtypeStruct((OCC * VL, QH), F32),
        in_specs=[pl.BlockSpec(memory_space=pltpu.VMEM)] * len(args),
        out_specs=pl.BlockSpec(memory_space=pltpu.VMEM),
        scratch_shapes=[pltpu.VMEM((width, QH), F32)],
        name=name,
    )(*args)


def density_last(places, own, other, row_term, col_term, cols, before, name):
    width = half_shards(cols) * 48
    count = len(cols)

    def kernel(places, *refs):
        inputs = refs[: 4 + count]
        before = refs[4 + count]
        sent_0, sent_1, kept_0, kept_1, whole, right = refs[5 + count :]
        term = before[...] + density_term((*inputs, right), count)
        order = (places[4], places[1], places[2], places[3])
        for q in range(QT):
            for i in range(OCC):
                for k in range(4):
                    row = (i * 4 + k) * 16
                    whole[q, i, order[k]] = term[row : row + 16, 128 * q : 128 * q + 128]
        low = lanes(32)
        low_all = lanes(VL)
        for target, start, slots in (
            (sent_0, 0, (1, 3)), (sent_1, 3, (2, 3)), (kept_0, 0, (0, 2)), (kept_1, 3, (0, 1)),
        ):
            for slot, k in enumerate(slots):
                y = order[k]
                for i in range(3):
                    for q in range(2):
                        row = (q * 3 + i) * VL
                        target[slot, row : row + VL, :] = whole[2 * y + q, start + i].reshape(VL, 128)
                    rest = whole[8 + y // 2, start + i].reshape(VL, 128)
                    rest = jnp.where(y % 2 == 1, half_turn(rest), rest)
                    row = 6 * VL + 32 * i
                    target[slot, row : row + 32, :] = jnp.where(low, rest[:32], half_turn(rest[32:]))

    piece = jax.ShapeDtypeStruct((2, 480, 128), F32)
    return pl.pallas_call(
        kernel,
        out_shape=(piece,) * 4,
        in_specs=[pl.BlockSpec(memory_space=pltpu.SMEM)] + [pl.BlockSpec(memory_space=pltpu.VMEM)] * (5 + count),
        out_specs=(pl.BlockSpec(memory_space=pltpu.VMEM),) * 4,
        scratch_shapes=[pltpu.VMEM((QT, OCC, 4, 16, 128), F32), pltpu.VMEM((width, QH), F32)],
        name=name,
    )(places, own, other, row_term, col_term, *cols, before)


def unpack_kernel(places, kept_0, near_0, last_0, kept_1, near_1, last_1, result):
    low = lanes(VL)
    for half, refs in enumerate(((kept_0, near_0, last_0), (kept_1, near_1, last_1))):
        kept, near, last = refs
        total = kept[0] + near[0] + last[...]
        for i in range(3):
            first = total[i * VL : i * VL + VL]
            second = total[(3 + i) * VL : (4 + i) * VL]
            packed = total[6 * VL + 32 * i : 6 * VL + 32 * i + 32]
            rest = jnp.concatenate([packed, half_turn(packed)], axis=0)
            first_turned, second_turned = half_turn(first), half_turn(second)
            zero = places[0] == 0
            at = half * 3 + i
            result[at, :, 0:128] = jnp.where(zero, first, jnp.where(low, rest, first_turned))
            result[at, :, 128:256] = jnp.where(zero, second, jnp.where(low, first_turned, second_turned))
            result[at, :, 256:320] = jnp.where(zero, rest, second_turned)[:, :64]


def unpack(places, kept_0, near_0, last_0, kept_1, near_1, last_1):
    slot = pl.BlockSpec((1, 480, 128), lambda g: (0, 0, 0))
    whole = pl.BlockSpec((480, 128), lambda g: (0, 0))
    return pl.pallas_call(
        unpack_kernel,
        out_shape=jax.ShapeDtypeStruct((OCC, VL, QL), F32),
        in_specs=[pl.BlockSpec(memory_space=pltpu.SMEM), slot, slot, whole, slot, slot, whole],
        out_specs=pl.BlockSpec((OCC, VL, QL), lambda g: (0, 0, 0)),
        grid=(1,),
        name="unpack",
    )(places, kept_0, near_0, last_0, kept_1, near_1, last_1)


def pick(table, places):
    at = jnp.arange(table.shape[0], dtype=jnp.int32)
    return jnp.sum(jnp.where(places[:, None] == at[None, :], table[None, :], 0), axis=1)


def reduce_pieces(sent_0, sent_1, kept_0, kept_1):
    near_0 = on_aux(sent_0, YA)
    near_1 = on_aux(sent_1, YB)
    last_0 = on_aux(kept_0[1] + near_0[1], YB)
    last_1 = on_aux(kept_1[1] + near_1[1], YA)
    return near_0, near_1, last_0, last_1


def shards(integrals, metric_root, occ_energy, virt_energy, batch_index, virt_order):
    aux_place = lax.axis_index("aux").astype(jnp.int32)
    virt_place = lax.axis_index("virt").astype(jnp.int32)
    y, core = aux_place // 2, aux_place % 2
    z, x = virt_place // 4, virt_place % 4
    near = [y ^ 1, 3 - y, (y + 2) % 4, y]
    places = jnp.stack([core, *near])
    partner_places = jnp.stack([1 - core, *near])

    values = integrals.transpose(1, 0, 2)
    metric = metric_root.T
    out_sent, out_kept = fitted_part(partner_places, values, metric, "fitted_for_partner")
    in_sent = on_aux(out_sent, CORE)
    in_kept = on_aux(out_kept, CORE)
    own_sent, own_kept = fitted_part(places, values, metric, "fitted_for_self")
    sent_0, sent_1 = own_sent[0] + in_sent[0], own_sent[1] + in_sent[1]
    kept_0, kept_1 = own_kept[0] + in_kept[0], own_kept[1] + in_kept[1]
    near_0, near_1, last_0, last_1 = reduce_pieces(sent_0, sent_1, kept_0, kept_1)
    half_0 = kept_0[0] + near_0[0] + last_0
    half_1 = kept_1[0] + near_1[0] + last_1

    a_m, a_p, a_2 = on_virt(half_0, XP), on_virt(half_0, XM), on_virt(half_0, X2)
    b_m, b_p, b_2 = on_virt(half_1, ZP), on_virt(half_1, ZM), on_virt(half_1, Z2)
    own = jnp.stack([half_0, half_1])
    row_a, row_b = on_aux(own, YA), on_aux(own, YB)
    far_0, far_1 = on_aux(row_a[0], YB), on_aux(row_b[1], YA)
    rows = (own, row_a, row_b, far_0, far_1)

    u_a, w_a = jnp.stack([half_0, a_m]), jnp.stack([a_p, a_2])
    u_b, w_b = jnp.stack([half_1, b_m]), jnp.stack([b_p, b_2])
    ua_m, ua_p = on_virt(u_a, ZP), on_virt(u_a, ZM)
    ub_m, ub_p = on_virt(u_b, XP), on_virt(u_b, XM)
    wa_m, wa_p = on_virt(w_a, ZP), on_virt(w_a, ZM)
    wb_m, wb_p = on_virt(w_b, XP), on_virt(w_b, XM)
    ua_2, wa_2 = on_virt(ua_m, ZP), on_virt(wa_p, ZM)
    ub_2, wb_2 = on_virt(ub_m, XP), on_virt(wb_p, XM)

    first = (u_a, w_a, u_b, w_b)
    second = (ua_m, wa_m, ua_p, wa_p, ub_m, wb_m, ub_p, wb_p)
    third = (ua_2, wa_2, ub_2, wb_2)
    turn = (0, -1, 1, 2)
    spots = (
        [(0, d, 0) for d in turn] + [(d, 0, 1) for d in turn],
        [(s, d, 0) for s in (-1, 1) for d in turn] + [(d, s, 1) for s in (-1, 1) for d in turn],
        [(2, d, 0) for d in turn] + [(d, 2, 1) for d in turn],
    )

    eight = jnp.arange(8, dtype=jnp.int32)
    row_spots = [virt_place * VL + r * 16 + h * 8 + eight for r in (y, near[0], near[1], near[2]) for h in range(2)]
    col_spots = [
        ((z + dz) % 4 * 4 + (x + dx) % 4) * VL + y * 16 + h * 8 + eight for part in spots for dz, dx, h in part
    ]
    entries = pick(virt_order, jnp.concatenate(row_spots + col_spots))
    levels = pick(virt_energy, entries)
    occ = pick(occ_energy, batch_index)
    terms = occ[:, None] - levels[None, :]
    row_term = terms[:, :64].reshape(OCC * VL, 1)
    col_terms = [terms[:, a:b].reshape(1, -1) for a, b in ((64, 128), (128, 256), (256, 320))]

    pair_1 = pair_part(rows, first, "pair_first")
    other_1 = on_aux(pair_1, CORE)
    sum_1 = density_part(pair_1, other_1, row_term, col_terms[0], first, None, "density_first")
    pair_2 = pair_part(rows, second, "pair_second")
    other_2 = on_aux(pair_2, CORE)
    sum_2 = density_part(pair_2, other_2, row_term, col_terms[1], second, sum_1, "density_second")
    pair_3 = pair_part(rows, third, "pair_third")
    other_3 = on_aux(pair_3, CORE)
    out_0, out_1, stay_0, stay_1 = density_last(
        places, pair_3, other_3, row_term, col_terms[2], third, sum_2, "density_third"
    )
    near_0, near_1, last_0, last_1 = reduce_pieces(out_0, out_1, stay_0, stay_1)
    result = unpack(places, stay_0, near_0, last_0, stay_1, near_1, last_1)
    return result.transpose(1, 0, 2)


def solution(mesh):
    return jax.shard_map(
        shards,
        mesh=mesh,
        in_specs=(P("virt", None, "aux"), P(None, "aux"), P(), P(), P(), P()),
        out_specs=P("virt", None, "aux"),
        check_vma=False,
    )
```

```python
import jax
import jax.numpy as jnp
import numpy as np
from jax import lax
from jax.experimental import pallas as pl
from jax.experimental.pallas import tpu as pltpu
from jax.sharding import PartitionSpec as P


F32 = jnp.float32
BF16 = jnp.bfloat16
OCC = 6
VL = 64
QL = 320
QH = 1280
QT = QH // 128


def plane(dz, dx):
    return [(z * 4 + x, (z + dz) % 4 * 4 + (x + dx) % 4) for z in range(4) for x in range(4)]


def column(place, swap):
    return [(y * 2 + c, place(y) * 2 + (c ^ swap)) for y in range(4) for c in range(2)]


XP, XM, X2 = plane(0, 1), plane(0, -1), plane(0, 2)
ZP, ZM, Z2 = plane(1, 0), plane(-1, 0), plane(2, 0)
YA = column(lambda y: y ^ 1, 0)
YB = column(lambda y: 3 - y, 0)
CORE = column(lambda y: y, 1)


def split(value):
    high = value.astype(BF16)
    return high, (value - high.astype(F32)).astype(BF16)


def product(left, right, dims):
    left_high, left_low = left
    right_high, right_low = right

    def one(a, b):
        return lax.dot_general(a, b, (dims, ((), ())), preferred_element_type=F32)

    return one(left_high, right_low) + one(left_low, right_high) + one(left_high, right_high)


def half_turn(value):
    return pltpu.roll(value, 64, 1)


def lanes(rows):
    return lax.broadcasted_iota(jnp.int32, (rows, 128), 1) < 64


def fitted_kernel(places, integrals, metric, sent, kept, right, full):
    core = places[0]
    for y in range(4):
        start = pl.multiple_of(640 * y + 384 * core, 128)
        right[:, 256 * y : 256 * y + 256] = metric[:, pl.ds(start, 256)]
    low = lanes(QL)
    for p in range(2):
        first = metric[:, 1280 * p + 256 : 1280 * p + 384]
        second = metric[:, 1280 * p + 896 : 1280 * p + 1024]
        even = jnp.where(low, first, half_turn(second))
        odd = jnp.where(low, half_turn(first), second)
        right[:, 1024 + 128 * p : 1152 + 128 * p] = jnp.where(core == 0, even, odd)
    left = integrals[...].reshape(OCC * VL, QL)
    value = product(split(left), split(right[...]), ((1,), (0,)))
    full[...] = value.reshape(OCC, 4, 2, 8, QH)
    y_a, y_b, y_far, y_own = places[1], places[2], places[3], places[4]
    for target, half, slot, y in (
        (sent, 0, 0, y_a), (sent, 0, 1, y_far), (sent, 1, 0, y_b), (sent, 1, 1, y_far),
        (kept, 0, 0, y_own), (kept, 0, 1, y_b), (kept, 1, 0, y_own), (kept, 1, 1, y_a),
    ):
        for i in range(OCC):
            for q in range(QT):
                target[half, slot, i, q] = full[i, y, half, :, 128 * q : 128 * q + 128]


def fitted_part(places, integrals, metric):
    piece = jax.ShapeDtypeStruct((2, 2, OCC, QT, 8, 128), F32)
    return pl.pallas_call(
        fitted_kernel,
        out_shape=(piece, piece),
        in_specs=[
            pl.BlockSpec(memory_space=pltpu.SMEM),
            pl.BlockSpec(memory_space=pltpu.VMEM),
            pl.BlockSpec(memory_space=pltpu.VMEM),
        ],
        out_specs=(pl.BlockSpec(memory_space=pltpu.VMEM),) * 2,
        scratch_shapes=[pltpu.VMEM((QL, QH), F32), pltpu.VMEM((OCC, 4, 2, 8, QH), F32)],
        compiler_params=settings(20),
        cost_estimate=cost(FLOPS // 3),
    )(places, integrals, metric)


def store_split(high, low, row, q, first, second):
    value = jnp.concatenate([first, second], axis=0)
    upper, lower = split(value)
    high[row : row + 16, 128 * q : 128 * q + 128] = upper
    low[row : row + 16, 128 * q : 128 * q + 128] = lower


VMEM_SPEC = pl.BlockSpec(memory_space=pltpu.VMEM)
SMEM_SPEC = pl.BlockSpec(memory_space=pltpu.SMEM)
PARTS = (jax.ShapeDtypeStruct((OCC * VL, QH), BF16),) * 2
FLOPS = 2 * 3 * (OCC * VL) ** 2 * QH


def settings(mebibytes):
    return pltpu.CompilerParams(vmem_limit_bytes=mebibytes * 2**20)


def cost(flops):
    return pl.CostEstimate(flops=flops, bytes_accessed=4 * 2**20, transcendentals=0)


def rows_kernel(own, near_a, near_b, far_0, far_1, high, low):
    for i in range(OCC):
        for k, ref in enumerate((own, near_a, near_b, None)):
            for q in range(QT):
                first, second = (far_0[i, q], far_1[i, q]) if ref is None else (ref[0, i, q], ref[1, i, q])
                store_split(high, low, (i * 4 + k) * 16, q, first, second)


def rows_part(*rows):
    return pl.pallas_call(
        rows_kernel,
        out_shape=PARTS,
        in_specs=[VMEM_SPEC] * 5,
        out_specs=(VMEM_SPEC,) * 2,
        compiler_params=settings(12),
        cost_estimate=cost(FLOPS // 4),
        name="rows",
    )(*rows)


def pair_kernel(left_high, left_low, *refs):
    cols = refs[:4]
    result, high, low = refs[4:]
    for i in range(OCC):
        for k, ref in enumerate(cols):
            for q in range(QT):
                store_split(high, low, (i * 4 + k) * 16, q, ref[0, i, q], ref[1, i, q])
    left = left_high[...], left_low[...]
    result[...] = product(left, (high[...], low[...]), ((1,), (1,)))


def pair_part(left, cols):
    return pl.pallas_call(
        pair_kernel,
        out_shape=(jax.ShapeDtypeStruct((OCC * VL, OCC * VL), F32), *PARTS),
        in_specs=[VMEM_SPEC] * 6,
        out_specs=(VMEM_SPEC,) * 3,
        compiler_params=settings(16),
        cost_estimate=cost(FLOPS),
    )(*left, *cols)


def amplitudes(pair, row_term, col_term):
    low = lanes(VL)
    pieces = []
    for i in range(OCC):
        at = 128 * (i // 2)
        swapped = []
        for t in range(OCC // 2):
            first = pair[2 * t * VL : 2 * t * VL + VL, at : at + 128]
            second = pair[(2 * t + 1) * VL : (2 * t + 2) * VL, at : at + 128]
            if i % 2 == 0:
                second = half_turn(second)
            else:
                first = half_turn(first)
            swapped.append(jnp.where(low, first, second))
        direct = pair[VL * i : VL * i + VL, :]
        levels = row_term[VL * i : VL * i + VL, :] + col_term
        pieces.append((2.0 * direct - jnp.concatenate(swapped, axis=1)) / levels)
    return jnp.concatenate(pieces, axis=0)


def density_term(own, other, row_term, col_term, high, low):
    amplitude = amplitudes(own[...] + other[...], row_term[...], col_term[...])
    return product(split(amplitude), (high[...], low[...]), ((1,), (0,)))


def density_first_kernel(*refs):
    refs[-1][...] = density_term(*refs[:-1])


def density_next_kernel(*refs):
    refs[-1][...] = refs[-2][...] + density_term(*refs[:-2])


def density_part(inputs, before):
    args = inputs if before is None else (*inputs, before)
    return pl.pallas_call(
        density_first_kernel if before is None else density_next_kernel,
        out_shape=jax.ShapeDtypeStruct((OCC * VL, QH), F32),
        in_specs=[VMEM_SPEC] * len(args),
        out_specs=VMEM_SPEC,
        compiler_params=settings(16),
        cost_estimate=cost(FLOPS),
    )(*args)


def density_last_kernel(places, *refs):
    before, sent_0, sent_1, kept_0, kept_1, whole = refs[6:]
    term = before[...] + density_term(*refs[:6])
    order = (places[4], places[1], places[2], places[3])
    for q in range(QT):
        for i in range(OCC):
            for k in range(4):
                row = (i * 4 + k) * 16
                whole[q, i, order[k]] = term[row : row + 16, 128 * q : 128 * q + 128]
    low = lanes(32)
    for target, start, slots in (
        (sent_0, 0, (1, 3)), (sent_1, 3, (2, 3)), (kept_0, 0, (0, 2)), (kept_1, 3, (0, 1)),
    ):
        for slot, k in enumerate(slots):
            y = order[k]
            for i in range(3):
                for q in range(2):
                    row = (q * 3 + i) * VL
                    target[slot, row : row + VL, :] = whole[2 * y + q, start + i].reshape(VL, 128)
                rest = whole[8 + y // 2, start + i].reshape(VL, 128)
                rest = jnp.where(y % 2 == 1, half_turn(rest), rest)
                row = 6 * VL + 32 * i
                target[slot, row : row + 32, :] = jnp.where(low, rest[:32], half_turn(rest[32:]))


def density_last(places, inputs, before):
    piece = jax.ShapeDtypeStruct((2, 480, 128), F32)
    return pl.pallas_call(
        density_last_kernel,
        out_shape=(piece,) * 4,
        in_specs=[SMEM_SPEC] + [VMEM_SPEC] * 7,
        out_specs=(VMEM_SPEC,) * 4,
        scratch_shapes=[pltpu.VMEM((QT, OCC, 4, 16, 128), F32)],
        compiler_params=settings(18),
        cost_estimate=cost(FLOPS),
    )(places, *inputs, before)


def unpack_kernel(places, kept_0, near_0, last_0, kept_1, near_1, last_1, result):
    low = lanes(VL)
    for half, refs in enumerate(((kept_0, near_0, last_0), (kept_1, near_1, last_1))):
        kept, near, last = refs
        total = kept[0] + near[0] + last[...]
        for i in range(3):
            first = total[i * VL : i * VL + VL]
            second = total[(3 + i) * VL : (4 + i) * VL]
            packed = total[6 * VL + 32 * i : 6 * VL + 32 * i + 32]
            rest = jnp.concatenate([packed, half_turn(packed)], axis=0)
            first_turned, second_turned = half_turn(first), half_turn(second)
            zero = places[0] == 0
            at = half * 3 + i
            result[at, :, 0:128] = jnp.where(zero, first, jnp.where(low, rest, first_turned))
            result[at, :, 128:256] = jnp.where(zero, second, jnp.where(low, first_turned, second_turned))
            result[at, :, 256:320] = jnp.where(zero, rest, second_turned)[:, :64]


def unpack(places, kept_0, near_0, last_0, kept_1, near_1, last_1):
    slot = pl.BlockSpec((1, 480, 128), lambda g: (0, 0, 0))
    whole = pl.BlockSpec((480, 128), lambda g: (0, 0))
    return pl.pallas_call(
        unpack_kernel,
        out_shape=jax.ShapeDtypeStruct((OCC, VL, QL), F32),
        in_specs=[pl.BlockSpec(memory_space=pltpu.SMEM), slot, slot, whole, slot, slot, whole],
        out_specs=pl.BlockSpec((OCC, VL, QL), lambda g: (0, 0, 0)),
        grid=(1,),
        compiler_params=settings(10),
        name="unpack",
    )(places, kept_0, near_0, last_0, kept_1, near_1, last_1)


def pick(table, places):
    at = jnp.arange(table.shape[0], dtype=jnp.int32)
    return jnp.sum(jnp.where(places[:, None] == at[None, :], table[None, :], 0), axis=1)


def on_virt(value, pairs):
    return lax.ppermute(value, "virt", pairs)


def on_aux(value, pairs):
    return lax.ppermute(value, "aux", pairs)


def stacked(first, second):
    return jnp.stack([first, second])


SPOTS = (
    (0, 0, 0), (0, -1, 0), (0, 1, 0), (0, 2, 0), (0, 0, 1), (-1, 0, 1), (1, 0, 1), (2, 0, 1),
    (-1, 0, 0), (-1, -1, 0), (1, 0, 0), (1, -1, 0), (0, -1, 1), (-1, -1, 1), (0, 1, 1), (-1, 1, 1),
    (-1, 1, 0), (-1, 2, 0), (1, 1, 0), (1, 2, 0), (1, -1, 1), (2, -1, 1), (1, 1, 1), (2, 1, 1),
    (2, 0, 0), (2, -1, 0), (2, 1, 0), (2, 2, 0), (0, 2, 1), (-1, 2, 1), (1, 2, 1), (2, 2, 1),
)


def spread(values):
    return jnp.asarray(np.repeat(np.asarray(values, np.int32), 8))


def energy_terms(y, z, x, near, occ_energy, virt_energy, batch_index, virt_order):
    eight = jnp.asarray(np.tile(np.arange(8, dtype=np.int32), 40))
    zeros = [0] * 8
    step_z = spread(zeros + [s[0] for s in SPOTS])
    step_x = spread(zeros + [s[1] for s in SPOTS])
    half = spread([0, 1] * 4 + [s[2] for s in SPOTS])
    turn = spread([0, 0, 1, 1, 2, 2, 3, 3] + [0] * 32)
    chip = jnp.where(turn == 0, y, jnp.where(turn == 1, near[0], jnp.where(turn == 2, near[1], near[2])))
    spots = (((z + step_z) & 3) * 4 + ((x + step_x) & 3)) * VL + chip * 16 + half * 8 + eight
    levels = pick(virt_energy, pick(virt_order, spots))
    terms = pick(occ_energy, batch_index)[:, None] - levels[None, :]
    row_term = terms[:, :64].reshape(OCC * VL, 1)
    return row_term, [terms[:, 64 * k : 64 * k + 64].reshape(1, OCC * VL) for k in range(1, 5)]


def shards(integrals, metric_root, occ_energy, virt_energy, batch_index, virt_order):
    aux_place = lax.axis_index("aux").astype(jnp.int32)
    virt_place = lax.axis_index("virt").astype(jnp.int32)
    y, core = aux_place // 2, aux_place % 2
    z, x = virt_place // 4, virt_place % 4
    near = [y ^ 1, 3 - y, (y + 2) % 4, y]
    places = jnp.stack([core, *near])
    partner_places = jnp.stack([1 - core, *near])

    values = integrals.transpose(1, 0, 2)
    metric = metric_root.T
    out_sent, out_kept = fitted_part(partner_places, values, metric)
    in_sent = on_aux(out_sent, CORE)
    in_kept = on_aux(out_kept, CORE)
    own_sent, own_kept = fitted_part(places, values, metric)
    sent_0, sent_1 = own_sent[0] + in_sent[0], own_sent[1] + in_sent[1]
    kept_0, kept_1 = own_kept[0] + in_kept[0], own_kept[1] + in_kept[1]
    near_0 = on_aux(sent_0, YA)
    near_1 = on_aux(sent_1, YB)
    row_term, col_terms = energy_terms(y, z, x, near, occ_energy, virt_energy, batch_index, virt_order)
    near_0, near_1, row_term, col_terms = lax.optimization_barrier((near_0, near_1, row_term, col_terms))
    last_0 = on_aux(kept_0[1] + near_0[1], YB)
    last_1 = on_aux(kept_1[1] + near_1[1], YA)
    half_0 = kept_0[0] + near_0[0] + last_0
    half_1 = kept_1[0] + near_1[0] + last_1

    a_m = on_virt(half_0, XP)
    a_p = on_virt(half_0, XM)
    b_m = on_virt(half_1, ZP)
    b_p = on_virt(half_1, ZM)
    own = stacked(half_0, half_1)
    row_a = on_aux(own, YA)
    row_b = on_aux(own, YB)
    a_2 = on_virt(half_0, X2)
    b_2 = on_virt(half_1, Z2)
    far_0 = on_aux(row_a[0], YB)
    far_1 = on_aux(row_b[1], YA)

    u_a, u_b = stacked(half_0, a_m), stacked(half_1, b_m)
    ua_m, ua_p = on_virt(u_a, ZP), on_virt(u_a, ZM)
    ub_m, ub_p = on_virt(u_b, XP), on_virt(u_b, XM)
    w_a, w_b = stacked(a_p, a_2), stacked(b_p, b_2)
    wa_m, wa_p = on_virt(w_a, ZP), on_virt(w_a, ZM)
    wb_m, wb_p = on_virt(w_b, XP), on_virt(w_b, XM)
    ua_2, ub_2 = on_virt(ua_m, ZP), on_virt(ub_m, XP)
    wa_2, wb_2 = on_virt(wa_p, ZM), on_virt(wb_p, XM)

    left = rows_part(own, row_a, row_b, far_0, far_1)
    chunks = (
        (u_a, w_a, u_b, w_b), (ua_m, ua_p, ub_m, ub_p), (wa_m, wa_p, wb_m, wb_p), (ua_2, wa_2, ub_2, wb_2),
    )
    total = None
    for k, cols in enumerate(chunks):
        pair, high, low = pair_part(left, cols)
        other = on_aux(pair, CORE)
        inputs = (pair, other, row_term, col_terms[k], high, low)
        if k < 3:
            total = density_part(inputs, total)
    out_0, out_1, stay_0, stay_1 = density_last(places, inputs, total)
    near_0 = on_aux(out_0, YA)
    near_1 = on_aux(out_1, YB)
    last_0 = on_aux(stay_0[1] + near_0[1], YB)
    last_1 = on_aux(stay_1[1] + near_1[1], YA)
    result = unpack(places, stay_0, near_0, last_0, stay_1, near_1, last_1)
    return result.transpose(1, 0, 2)


def solution(mesh):
    return jax.shard_map(
        shards,
        mesh=mesh,
        in_specs=(P("virt", None, "aux"), P(None, "aux"), P(), P(), P(), P()),
        out_specs=P("virt", None, "aux"),
        check_vma=False,
    )
```

```python
import jax
import jax.numpy as jnp
from jax import lax
from jax.experimental import pallas as pl
from jax.experimental.pallas import tpu as pltpu
from jax.sharding import PartitionSpec as P


F32 = jnp.float32
BF16 = jnp.bfloat16
OCC = 6
VL = 64
QL = 320
QH = 1280
QT = QH // 128


def plane(step_z, step_x):
    return [(z * 4 + x, (z ^ step_z) * 4 + (x ^ step_x)) for z in range(4) for x in range(4)]


def column(place, swap):
    return [(y * 2 + c, place(y) * 2 + (c ^ swap)) for y in range(4) for c in range(2)]


XA, XB = plane(0, 1), plane(0, 3)
ZA, ZB = plane(1, 0), plane(3, 0)
YA = column(lambda y: y ^ 1, 0)
YB = column(lambda y: y ^ 3, 0)
Y2 = column(lambda y: y ^ 2, 0)
CORE = column(lambda y: y, 1)


def split(value):
    high = value.astype(BF16)
    return high, (value - high.astype(F32)).astype(BF16)


def product(left, right, dims):
    left_high, left_low = left
    right_high, right_low = right

    def one(a, b):
        return lax.dot_general(a, b, (dims, ((), ())), preferred_element_type=F32)

    return one(left_high, right_low) + one(left_low, right_high) + one(left_high, right_high)


def half_turn(value):
    return pltpu.roll(value, 64, 1)


def lanes(rows):
    return lax.broadcasted_iota(jnp.int32, (rows, 128), 1) < 64


VMEM_SPEC = pl.BlockSpec(memory_space=pltpu.VMEM)
SMEM_SPEC = pl.BlockSpec(memory_space=pltpu.SMEM)
HBM_SPEC = pl.BlockSpec(memory_space=pltpu.HBM)
PIECE = (OCC, QT, 8, 128)
PART = (OCC * VL, QH)
FLOPS = 2 * 3 * (OCC * VL) ** 2 * QH


def settings(mebibytes):
    return pltpu.CompilerParams(vmem_limit_bytes=mebibytes * 2**20)


def cost(flops):
    return pl.CostEstimate(flops=flops, bytes_accessed=4 * 2**20, transcendentals=0)


def near_memory(shape, kind=F32):
    return pltpu.VMEM(shape, kind)


def held(*values):
    return [pltpu.with_memory_space_constraint(v, pltpu.VMEM) for v in values]


def fitted_kernel(places, integrals, metric, sent, kept, left, right, full, arrivals):
    core = places[0]
    start = pl.multiple_of(256 * core, 128)
    copies = [pltpu.make_async_copy(integrals, left, arrivals.at[4])]
    for y in range(4):
        columns = metric.at[:, pl.ds(pl.multiple_of(640 * y + start, 128), 384)]
        copies.append(pltpu.make_async_copy(columns, right.at[y], arrivals.at[y]))
    for copy in copies:
        copy.start()
    copies[0].wait()
    rows = left[...].reshape(OCC * VL, QL)
    main_high, main_low = split(rows[:, :256])
    rest_high, rest_low = split(rows[:, 256:])
    rest = jnp.concatenate([rest_high, rest_low, rest_high], axis=1)
    side = pl.multiple_of(128 * core, 128)
    other = pl.multiple_of(256 - 256 * core, 128)
    low = lanes(QL)

    def put(columns, at):
        high, low_part = split(columns)
        value = product((main_high, main_low), (high[:256], low_part[:256]), ((1,), (0,)))
        ends = jnp.concatenate([low_part[256:], high[256:], high[256:]], axis=0)
        value = value + jnp.dot(rest, ends, preferred_element_type=F32)
        full[:, :, :, :, at : at + 256] = value.reshape(OCC, 4, 2, 8, 256)

    rests = []
    for y in range(4):
        copies[1 + y].wait()
        put(right[y, :, pl.ds(side, 256)], 256 * y)
        rests.append(right[y, :, pl.ds(other, 128)])
    packed = []
    for p in range(2):
        first, second = rests[2 * p], rests[2 * p + 1]
        even = jnp.where(low, first, half_turn(second))
        odd = jnp.where(low, half_turn(first), second)
        packed.append(jnp.where(core == 0, even, odd))
    put(jnp.concatenate(packed, axis=1), 1024)
    y_a, y_b, y_far, y_own = places[1], places[2], places[3], places[4]
    for target, half, slot, y in (
        (sent, 0, 0, y_a), (sent, 0, 1, y_far), (sent, 1, 0, y_b), (sent, 1, 1, y_far),
        (kept, 0, 0, y_own), (kept, 0, 1, y_b), (kept, 1, 0, y_own), (kept, 1, 1, y_a),
    ):
        for i in range(OCC):
            for q in range(QT):
                target[half, slot, i, q] = full[i, y, half, :, 128 * q : 128 * q + 128]


def fitted_part(places, integrals, metric):
    piece = near_memory((2, 2, *PIECE))
    return pl.pallas_call(
        fitted_kernel,
        out_shape=(piece, piece),
        in_specs=[SMEM_SPEC, HBM_SPEC, HBM_SPEC],
        out_specs=(VMEM_SPEC,) * 2,
        scratch_shapes=[
            pltpu.VMEM((OCC, VL, QL), F32),
            pltpu.VMEM((4, QL, 384), F32),
            pltpu.VMEM((OCC, 4, 2, 8, QH), F32),
            pltpu.SemaphoreType.DMA((5,)),
        ],
        compiler_params=settings(12),
        cost_estimate=cost(FLOPS // 3),
    )(places, integrals, metric)


def small_call(kernel, shapes, args):
    return pl.pallas_call(
        kernel,
        out_shape=tuple(near_memory(shape) for shape in shapes),
        in_specs=[VMEM_SPEC] * len(args),
        out_specs=(VMEM_SPEC,) * len(shapes),
        compiler_params=settings(4),
        cost_estimate=cost(FLOPS // 40),
    )(*held(*args))


def sent_kernel(own, other, near_0, near_1, far_0, far_1):
    for half, near, far in ((0, near_0, far_0), (1, near_1, far_1)):
        near[...] = own[half, 0] + other[half, 0]
        far[...] = own[half, 1] + other[half, 1]


def relay_kernel(half):
    def kernel(own, other, far, result):
        result[...] = own[half, 1] + other[half, 1] + far[...]

    return kernel


def shard_kernel(own, other, near_0, near_1, last_0, last_1, result):
    for half, near, last in ((0, near_0, last_0), (1, near_1, last_1)):
        result[half] = own[half, 0] + other[half, 0] + near[...] + last[...]


def line_kernel(half):
    def kernel(first, second, line):
        line[0], line[1] = first[half], second[half]

    return kernel


def join_kernel(half):
    def kernel(near, far, result):
        result[0], result[1] = near[half], far[...]

    return kernel


def pick_kernel(half):
    def kernel(value, result):
        result[...] = value[half]

    return kernel


def final_relay_kernel(kept, far, result):
    result[...] = kept[1] + far[...]


def store_split(high, low, row, q, first, second):
    value = jnp.concatenate([first, second], axis=0)
    upper, lower = split(value)
    high[row : row + 16, 128 * q : 128 * q + 128] = upper
    low[row : row + 16, 128 * q : 128 * q + 128] = lower


def rows_kernel(own, near_a, near_b, far, high, low):
    for i in range(OCC):
        for k, ref in enumerate((own, near_a, near_b, far)):
            for q in range(QT):
                store_split(high, low, (i * 4 + k) * 16, q, ref[0, i, q], ref[1, i, q])


def rows_part(*rows):
    return pl.pallas_call(
        rows_kernel,
        out_shape=(near_memory(PART, BF16),) * 2,
        in_specs=[VMEM_SPEC] * 4,
        out_specs=(VMEM_SPEC,) * 2,
        compiler_params=settings(4),
        cost_estimate=cost(FLOPS // 8),
        name="rows",
    )(*held(*rows))


def pair_kernel(left_high, left_low, *refs):
    cols = refs[:-3]
    result, high, low = refs[-3:]
    blocks = []
    for ref in cols:
        blocks += [(ref, ())] if len(ref.shape) == 4 else [(ref, (0,)), (ref, (1,))]
    count = len(blocks) // 2
    for i in range(OCC):
        for k in range(count):
            (one, at_one), (two, at_two) = blocks[2 * k], blocks[2 * k + 1]
            for q in range(QT):
                store_split(high, low, (i * count + k) * 16, q, one[(*at_one, i, q)], two[(*at_two, i, q)])
    left = left_high[...], left_low[...]
    result[...] = product(left, (high[...], low[...]), ((1,), (1,)))


def pair_part(left, cols):
    width = 48 * sum(1 if c.ndim == 4 else 2 for c in cols)
    part = near_memory((width, QH), BF16)
    return pl.pallas_call(
        pair_kernel,
        out_shape=(near_memory((OCC * VL, width)), part, part),
        in_specs=[VMEM_SPEC] * (2 + len(cols)),
        out_specs=(VMEM_SPEC,) * 3,
        compiler_params=settings(12),
        cost_estimate=cost(FLOPS),
    )(*held(*left, *cols))


def amplitudes(pair, row_term, col_term):
    low = lanes(VL)
    pieces = []
    for i in range(OCC):
        at = 128 * (i // 2)
        swapped = []
        if pair.shape[1] == 2 * OCC * VL:
            swapped = [pair[VL * j : VL * j + VL, 128 * i : 128 * i + 128] for j in range(OCC)]
        for t in range(0 if swapped else OCC // 2):
            first = pair[2 * t * VL : 2 * t * VL + VL, at : at + 128]
            second = pair[(2 * t + 1) * VL : (2 * t + 2) * VL, at : at + 128]
            if i % 2 == 0:
                second = half_turn(second)
            else:
                first = half_turn(first)
            swapped.append(jnp.where(low, first, second))
        direct = pair[VL * i : VL * i + VL, :]
        levels = row_term[VL * i : VL * i + VL, :] + col_term
        pieces.append((2.0 * direct - jnp.concatenate(swapped, axis=1)) / levels)
    return jnp.concatenate(pieces, axis=0)


def density_term(own, other, row_term, col_term, high, low):
    amplitude = amplitudes(own[...] + other[...], row_term[...], col_term[...])
    return product(split(amplitude), (high[...], low[...]), ((1,), (0,)))


def density_first_kernel(*refs):
    refs[-1][...] = density_term(*refs[:-1])


def density_next_kernel(*refs):
    refs[-1][...] = refs[-2][...] + density_term(*refs[:-2])


def density_part(inputs, before):
    args = inputs if before is None else (*inputs, before)
    return pl.pallas_call(
        density_first_kernel if before is None else density_next_kernel,
        out_shape=near_memory(PART),
        in_specs=[VMEM_SPEC] * len(args),
        out_specs=VMEM_SPEC,
        compiler_params=settings(10),
        cost_estimate=cost(FLOPS),
    )(*held(*args))


def density_last_kernel(places, *refs):
    before, near_0, near_1, far_0, far_1, kept_0, kept_1, whole = refs[6:]
    term = before[...] + density_term(*refs[:6])
    order = (places[4], places[1], places[2], places[3])
    for q in range(QT):
        for i in range(OCC):
            for k in range(4):
                row = (i * 4 + k) * 16
                whole[q, i, order[k]] = term[row : row + 16, 128 * q : 128 * q + 128]
    low = lanes(32)
    for target, start, k in (
        (far_0, 0, 3), (far_1, 3, 3), (near_0, 0, 1), (near_1, 3, 2),
        (kept_0.at[0], 0, 0), (kept_0.at[1], 0, 2), (kept_1.at[0], 3, 0), (kept_1.at[1], 3, 1),
    ):
        y = order[k]
        for i in range(3):
            for q in range(2):
                row = (q * 3 + i) * VL
                target[row : row + VL, :] = whole[2 * y + q, start + i].reshape(VL, 128)
            rest = whole[8 + (y >> 1), start + i].reshape(VL, 128)
            rest = jnp.where((y & 1) == 1, half_turn(rest), rest)
            row = 6 * VL + 32 * i
            target[row : row + 32, :] = jnp.where(low, rest[:32], half_turn(rest[32:]))


def density_last(places, inputs, before):
    piece, two = near_memory((480, 128)), near_memory((2, 480, 128))
    return pl.pallas_call(
        density_last_kernel,
        out_shape=(piece,) * 4 + (two,) * 2,
        in_specs=[SMEM_SPEC] + [VMEM_SPEC] * 7,
        out_specs=(VMEM_SPEC,) * 6,
        scratch_shapes=[pltpu.VMEM((QT, OCC, 4, 16, 128), F32)],
        compiler_params=settings(12),
        cost_estimate=cost(FLOPS),
    )(places, *held(*inputs, before))


def unpack_kernel(places, kept_0, near_0, last_0, kept_1, near_1, last_1, result):
    low = lanes(VL)
    for half, refs in enumerate(((kept_0, near_0, last_0), (kept_1, near_1, last_1))):
        kept, near, last = refs
        total = kept[0] + near[...] + last[...]
        for i in range(3):
            first = total[i * VL : i * VL + VL]
            second = total[(3 + i) * VL : (4 + i) * VL]
            packed = total[6 * VL + 32 * i : 6 * VL + 32 * i + 32]
            rest = jnp.concatenate([packed, half_turn(packed)], axis=0)
            first_turned, second_turned = half_turn(first), half_turn(second)
            zero = places[0] == 0
            at = half * 3 + i
            result[at, :, 0:128] = jnp.where(zero, first, jnp.where(low, rest, first_turned))
            result[at, :, 128:256] = jnp.where(zero, second, jnp.where(low, first_turned, second_turned))
            result[at, :, 256:320] = jnp.where(zero, rest, second_turned)[:, :64]


def unpack(places, *parts):
    return pl.pallas_call(
        unpack_kernel,
        out_shape=jax.ShapeDtypeStruct((OCC, VL, QL), F32),
        in_specs=[SMEM_SPEC] + [VMEM_SPEC] * 6,
        out_specs=VMEM_SPEC,
        compiler_params=settings(4),
        name="unpack",
    )(places, *held(*parts))


def on_virt(value, pairs):
    return lax.ppermute(value, "virt", pairs)


def on_aux(value, pairs):
    return lax.ppermute(value, "aux", pairs)


SPOTS = (
    (0, 1, 0), (0, 1, 1), (0, 3, 0), (0, 3, 1), (1, 0, 0), (1, 0, 1), (3, 0, 0), (3, 0, 1),
    (1, 1, 0), (1, 3, 0), (3, 1, 0), (3, 3, 0), (1, 1, 1), (3, 1, 1), (1, 3, 1), (3, 3, 1),
    (0, 0, 0), (0, 0, 1), (0, 2, 0), (2, 0, 1), (1, 2, 0), (3, 2, 0), (2, 1, 1), (2, 3, 1),
    (2, 1, 0), (2, 3, 0), (1, 2, 1), (3, 2, 1), (2, 0, 0), (2, 2, 0), (0, 2, 1), (2, 2, 1),
)


def terms_kernel(places, batch_index, occ_energy, virt_energy, virt_order, row_term, *col_terms):
    z, x = places[5], places[6]
    chips = (places[4], places[1], places[2], places[3])
    lane = lax.broadcasted_iota(jnp.int32, (8, 128), 1).astype(F32)
    step = lax.broadcasted_iota(jnp.int32, (8, 128), 0).astype(F32)
    order = virt_order[...].astype(F32)

    def pick(table, at):
        total = jnp.zeros((8, 128), F32)
        for r in range(8):
            total = total + jnp.where(at == lane + 128.0 * r, table[r : r + 1, :], 0.0)
        return jnp.sum(total, axis=1, keepdims=True)

    spots = [(z * 4 + x, chips[r], h) for r in range(4) for h in range(2)]
    spots += [((z ^ dz) * 4 + (x ^ dx), chips[0], h) for dz, dx, h in SPOTS]
    levels = []
    for place, chip, half in spots:
        first = (place * VL + chip * 16 + half * 8).astype(F32)
        levels.append(pick(virt_energy[...], pick(order, first + step)))
    occ = [occ_energy[batch_index[i]] for i in range(OCC)]
    rows = jnp.concatenate(levels[:8], axis=0)
    for i in range(OCC):
        row_term[VL * i : VL * i + VL, :] = occ[i] - rows
    low = lax.broadcasted_iota(jnp.int32, (1, 128), 1) < 64
    first, second, third = col_terms

    def along(values):
        both = jnp.concatenate(values, axis=0)
        flat = jnp.broadcast_to(both, (128, 128)).T[:8]
        return flat[:1], half_turn(flat)[:1]

    flat, turned = along(levels[16:32])
    for i in range(OCC):
        second[:, 128 * i : 128 * i + 128] = occ[i] - flat
    flat, turned = along(levels[8:16] + levels[32:40])
    for target, value in ((first, jnp.where(low, flat, turned)), (third, jnp.where(low, turned, flat))):
        for t in range(3):
            target[:, 128 * t : 128 * t + 128] = jnp.where(low, occ[2 * t], occ[2 * t + 1]) - value


def energy_terms(places, batch_index, occ_energy, virt_energy, virt_order):
    column = near_memory((1, OCC * VL))
    return pl.pallas_call(
        terms_kernel,
        out_shape=(near_memory((OCC * VL, 1)), column, near_memory((1, 2 * OCC * VL)), column),
        in_specs=[SMEM_SPEC] * 3 + [VMEM_SPEC] * 2,
        out_specs=(VMEM_SPEC,) * 4,
        compiler_params=settings(4),
        cost_estimate=cost(FLOPS // 4),
        name="terms",
    )(places, batch_index, occ_energy, virt_energy.reshape(8, 128), virt_order.reshape(8, 128))


def shards(integrals, metric_root, occ_energy, virt_energy, batch_index, virt_order):
    aux_place = lax.axis_index("aux").astype(jnp.int32)
    virt_place = lax.axis_index("virt").astype(jnp.int32)
    y, core = aux_place >> 1, aux_place & 1
    z, x = virt_place >> 2, virt_place & 3
    near = [y ^ 1, y ^ 3, y ^ 2, y, z, x]
    places = jnp.stack([core, *near])
    partner_places = jnp.stack([1 - core, *near])

    values = pltpu.with_memory_space_constraint(integrals.transpose(1, 0, 2), pltpu.HBM)
    metric = pltpu.with_memory_space_constraint(metric_root.T, pltpu.HBM)
    out_sent, out_kept = fitted_part(partner_places, values, metric)
    in_sent = on_aux(out_sent, CORE)
    in_kept = on_aux(out_kept, CORE)
    own_sent, own_kept = fitted_part(places, values, metric)
    near_0, near_1, far_0, far_1 = small_call(sent_kernel, (PIECE,) * 4, (own_sent, in_sent))
    far_0, far_1 = on_aux(far_0, YA), on_aux(far_1, YB)
    near_0, near_1 = on_aux(near_0, YA), on_aux(near_1, YB)
    row_term, *col_terms = energy_terms(places, batch_index, occ_energy, virt_energy, virt_order)
    (last_0,) = small_call(relay_kernel(0), (PIECE,), (own_kept, in_kept, far_0))
    last_0 = on_aux(last_0, YB)
    (last_1,) = small_call(relay_kernel(1), (PIECE,), (own_kept, in_kept, far_1))
    last_1 = on_aux(last_1, YA)
    last_1, row_term, col_terms = lax.optimization_barrier((last_1, row_term, col_terms))
    parts = (own_kept, in_kept, near_0, near_1, last_0, last_1)
    (own,) = small_call(shard_kernel, ((2, *PIECE),), parts)

    s_xa, s_xb = on_virt(own, XA), on_virt(own, XB)
    s_za, s_zb = on_virt(own, ZA), on_virt(own, ZB)
    row_a, row_b = on_aux(own, YA), on_aux(own, YB)
    (beyond_a,) = small_call(pick_kernel(0), (PIECE,), (s_xa,))
    (beyond_b,) = small_call(pick_kernel(1), (PIECE,), (s_za,))
    a_2, b_2 = on_virt(beyond_a, XB), on_virt(beyond_b, ZB)
    row_2 = on_aux(own, Y2)

    (line_a,) = small_call(line_kernel(0), ((2, *PIECE),), (s_xa, s_xb))
    pa_a, pa_b = on_virt(line_a, ZA), on_virt(line_a, ZB)
    (line_b,) = small_call(line_kernel(1), ((2, *PIECE),), (s_za, s_zb))
    pb_a, pb_b = on_virt(line_b, XA), on_virt(line_b, XB)
    qa_b, qa_a = on_virt(a_2, ZB), on_virt(a_2, ZA)
    qb_b, qb_a = on_virt(b_2, XB), on_virt(b_2, XA)
    pa_2, pb_2 = on_virt(pa_a, ZB), on_virt(pb_a, XB)
    (both_a,) = small_call(join_kernel(0), ((2, *PIECE),), (s_zb, qa_b))
    (both_b,) = small_call(join_kernel(1), ((2, *PIECE),), (s_xb, qb_b))
    f_a, f_b = on_virt(both_a, ZA), on_virt(both_b, XA)

    left = rows_part(own, row_a, row_b, row_2)
    chunks = (
        (s_xa, s_xb, s_za, s_zb),
        (pa_a, pa_b, pb_a, pb_b, own, a_2, b_2, qa_a, qa_b, qb_a, qb_b),
        (pa_2, pb_2, f_a, f_b),
    )
    total = None
    for k, cols in enumerate(chunks):
        pair, high, low = pair_part(left, cols)
        other = on_aux(pair, CORE)
        inputs = (pair, other, row_term, col_terms[k], high, low)
        if k < 2:
            total = density_part(inputs, total)
    near_0, near_1, far_0, far_1, kept_0, kept_1 = density_last(places, inputs, total)
    far_0, far_1 = on_aux(far_0, YA), on_aux(far_1, YB)
    near_0, near_1 = on_aux(near_0, YA), on_aux(near_1, YB)
    (last_0,) = small_call(final_relay_kernel, ((480, 128),), (kept_0, far_0))
    last_0 = on_aux(last_0, YB)
    (last_1,) = small_call(final_relay_kernel, ((480, 128),), (kept_1, far_1))
    last_1 = on_aux(last_1, YA)
    result = unpack(places, kept_0, near_0, last_0, kept_1, near_1, last_1)
    return result.transpose(1, 0, 2)


def solution(mesh):
    return jax.shard_map(
        shards,
        mesh=mesh,
        in_specs=(P("virt", None, "aux"), P(None, "aux"), P(), P(), P(), P()),
        out_specs=P("virt", None, "aux"),
        check_vma=False,
    )
```

```python
import jax
import jax.numpy as jnp
from jax import lax
from jax.experimental import pallas as pl
from jax.experimental.pallas import tpu as pltpu
from jax.sharding import PartitionSpec as P


F32 = jnp.float32
BF16 = jnp.bfloat16
OCC = 6
VL = 64
QL = 320
QH = 1280
QT = QH // 128


def plane(step_z, step_x):
    return [(z * 4 + x, (z ^ step_z) * 4 + (x ^ step_x)) for z in range(4) for x in range(4)]


def column(place, swap):
    return [(y * 2 + c, place(y) * 2 + (c ^ swap)) for y in range(4) for c in range(2)]


XA, XB = plane(0, 1), plane(0, 3)
ZA, ZB = plane(1, 0), plane(3, 0)
YA = column(lambda y: y ^ 1, 0)
YB = column(lambda y: y ^ 3, 0)
Y2 = column(lambda y: y ^ 2, 0)
CORE = column(lambda y: y, 1)


def split(value):
    high = value.astype(BF16)
    return high, (value - high.astype(F32)).astype(BF16)


def product(left, right, dims):
    left_high, left_low = left
    right_high, right_low = right

    def one(a, b):
        return lax.dot_general(a, b, (dims, ((), ())), preferred_element_type=F32)

    return one(left_high, right_low) + one(left_low, right_high) + one(left_high, right_high)


def half_turn(value):
    return pltpu.roll(value, 64, 1)


def lanes(rows):
    return lax.broadcasted_iota(jnp.int32, (rows, 128), 1) < 64


VMEM_SPEC = pl.BlockSpec(memory_space=pltpu.VMEM)
SMEM_SPEC = pl.BlockSpec(memory_space=pltpu.SMEM)
HBM_SPEC = pl.BlockSpec(memory_space=pltpu.HBM)
PIECE = (OCC, QT, 8, 128)
PART = (OCC * VL, QH)
FLOPS = 2 * 3 * (OCC * VL) ** 2 * QH


def settings(mebibytes):
    return pltpu.CompilerParams(vmem_limit_bytes=mebibytes * 2**20)


def cost(flops):
    return pl.CostEstimate(flops=flops, bytes_accessed=4 * 2**20, transcendentals=0)


def chip_column():
    place = lax.axis_index("aux").astype(jnp.int32)
    y = place >> 1
    return place & 1, (y ^ 1, y ^ 3, y ^ 2, y)


def near_memory(shape, kind=F32):
    return pltpu.VMEM(shape, kind)


def held(*values):
    return [pltpu.with_memory_space_constraint(v, pltpu.VMEM) for v in values]


def fitted_rows(left):
    rows = left[...].reshape(OCC * VL, QL)
    main_high, main_low = split(rows[:, :256])
    rest_high, rest_low = split(rows[:, 256:])
    return main_high, main_low, jnp.concatenate([rest_high, rest_low, rest_high], axis=1)


def fitted_products(core, ys, rows, right, ready, sent, kept, full):
    main_high, main_low, rest = rows
    side = pl.multiple_of(128 * core, 128)
    other = pl.multiple_of(256 - 256 * core, 128)
    low = lanes(QL)

    def put(columns, at):
        high, low_part = split(columns)
        value = product((main_high, main_low), (high[:256], low_part[:256]), ((1,), (0,)))
        ends = jnp.concatenate([low_part[256:], high[256:], high[256:]], axis=0)
        value = value + jnp.dot(rest, ends, preferred_element_type=F32)
        full[:, :, :, :, at : at + 256] = value.reshape(OCC, 4, 2, 8, 256)

    rests = []
    for y in range(4):
        ready(y)
        put(right[y, :, pl.ds(side, 256)], 256 * y)
        rests.append(right[y, :, pl.ds(other, 128)])
    packed = []
    for p in range(2):
        first, second = rests[2 * p], rests[2 * p + 1]
        even = jnp.where(low, first, half_turn(second))
        odd = jnp.where(low, half_turn(first), second)
        packed.append(jnp.where(core == 0, even, odd))
    put(jnp.concatenate(packed, axis=1), 1024)
    y_a, y_b, y_far, y_own = ys
    for target, half, slot, y in (
        (sent, 0, 0, y_a), (sent, 0, 1, y_far), (sent, 1, 0, y_b), (sent, 1, 1, y_far),
        (kept, 0, 0, y_own), (kept, 0, 1, y_b), (kept, 1, 0, y_own), (kept, 1, 1, y_a),
    ):
        for i in range(OCC):
            for q in range(QT):
                target[half, slot, i, q] = full[i, y, half, :, 128 * q : 128 * q + 128]


def partner_kernel(integrals, metric, sent, kept, left, own_right, right, full, arrivals):
    core, ys = chip_column()
    copies = [pltpu.make_async_copy(integrals, left, arrivals.at[8])]
    for k, (which, target) in enumerate(((1 - core, right), (core, own_right))):
        start = pl.multiple_of(256 * which, 128)
        for y in range(4):
            columns = metric.at[:, pl.ds(pl.multiple_of(640 * y + start, 128), 384)]
            copies.append(pltpu.make_async_copy(columns, target.at[y], arrivals.at[4 * k + y]))
    for copy in copies:
        copy.start()
    copies[0].wait()
    rows = fitted_rows(left)
    fitted_products(1 - core, ys, rows, right, lambda y: copies[1 + y].wait(), sent, kept, full)
    for copy in copies[5:]:
        copy.wait()


def self_kernel(left, right, sent, kept, full):
    core, ys = chip_column()
    fitted_products(core, ys, fitted_rows(left), right, lambda y: None, sent, kept, full)


COLUMNS = (4, QL, 384)


def fitted_parts(integrals, metric, between):
    piece = near_memory((2, 2, *PIECE))
    common = dict(compiler_params=settings(12), cost_estimate=cost(FLOPS // 3))
    sent, kept, left, right = pl.pallas_call(
        partner_kernel,
        out_shape=(piece, piece, near_memory((OCC, VL, QL)), near_memory(COLUMNS)),
        in_specs=[HBM_SPEC, HBM_SPEC],
        out_specs=(VMEM_SPEC,) * 4,
        scratch_shapes=[
            pltpu.VMEM(COLUMNS, F32),
            pltpu.VMEM((OCC, 4, 2, 8, QH), F32),
            pltpu.SemaphoreType.DMA((9,)),
        ],
        name="fitted_for_partner",
        **common,
    )(integrals, metric)
    received = between(sent, kept)
    own = pl.pallas_call(
        self_kernel,
        out_shape=(piece, piece),
        in_specs=[VMEM_SPEC] * 2,
        out_specs=(VMEM_SPEC,) * 2,
        scratch_shapes=[pltpu.VMEM((OCC, 4, 2, 8, QH), F32)],
        name="fitted_for_self",
        **common,
    )(*held(left, right))
    return received, own


def small_call(kernel, shapes, args):
    return pl.pallas_call(
        kernel,
        out_shape=tuple(near_memory(shape) for shape in shapes),
        in_specs=[VMEM_SPEC] * len(args),
        out_specs=(VMEM_SPEC,) * len(shapes),
        compiler_params=settings(4),
        cost_estimate=cost(FLOPS // 40),
    )(*held(*args))


def sent_kernel(own, other, near_0, near_1, far_0, far_1):
    for half, near, far in ((0, near_0, far_0), (1, near_1, far_1)):
        near[...] = own[half, 0] + other[half, 0]
        far[...] = own[half, 1] + other[half, 1]


def relay_kernel(half):
    def kernel(own, other, far, result):
        result[...] = own[half, 1] + other[half, 1] + far[...]

    return kernel


def shard_kernel(own, other, near_0, near_1, last_0, last_1, result):
    for half, near, last in ((0, near_0, last_0), (1, near_1, last_1)):
        result[half] = own[half, 0] + other[half, 0] + near[...] + last[...]


def line_kernel(half):
    def kernel(first, second, line):
        line[0], line[1] = first[half], second[half]

    return kernel


def join_kernel(half):
    def kernel(near, far, result):
        result[0], result[1] = near[half], far[...]

    return kernel


def pick_kernel(half):
    def kernel(value, result):
        result[...] = value[half]

    return kernel


def final_relay_kernel(kept, far, result):
    result[...] = kept[1] + far[...]


def store_split(high, low, row, q, first, second):
    value = jnp.concatenate([first, second], axis=0)
    upper, lower = split(value)
    high[row : row + 16, 128 * q : 128 * q + 128] = upper
    low[row : row + 16, 128 * q : 128 * q + 128] = lower


def rows_kernel(own, near_a, near_b, far, high, low):
    for i in range(OCC):
        for k, ref in enumerate((own, near_a, near_b, far)):
            for q in range(QT):
                store_split(high, low, (i * 4 + k) * 16, q, ref[0, i, q], ref[1, i, q])


def rows_part(*rows):
    return pl.pallas_call(
        rows_kernel,
        out_shape=(near_memory(PART, BF16),) * 2,
        in_specs=[VMEM_SPEC] * 4,
        out_specs=(VMEM_SPEC,) * 2,
        compiler_params=settings(4),
        cost_estimate=cost(FLOPS // 8),
        name="rows",
    )(*held(*rows))


def pair_kernel(left_high, left_low, *refs):
    cols = refs[:-3]
    result, high, low = refs[-3:]
    blocks = []
    for ref in cols:
        blocks += [(ref, ())] if len(ref.shape) == 4 else [(ref, (0,)), (ref, (1,))]
    count = len(blocks) // 2
    for i in range(OCC):
        for k in range(count):
            (one, at_one), (two, at_two) = blocks[2 * k], blocks[2 * k + 1]
            for q in range(QT):
                store_split(high, low, (i * count + k) * 16, q, one[(*at_one, i, q)], two[(*at_two, i, q)])
    left = left_high[...], left_low[...]
    result[...] = product(left, (high[...], low[...]), ((1,), (1,)))


def pair_part(left, cols):
    width = 48 * sum(1 if c.ndim == 4 else 2 for c in cols)
    part = near_memory((width, QH), BF16)
    return pl.pallas_call(
        pair_kernel,
        out_shape=(near_memory((OCC * VL, width)), part, part),
        in_specs=[VMEM_SPEC] * (2 + len(cols)),
        out_specs=(VMEM_SPEC,) * 3,
        compiler_params=settings(12),
        cost_estimate=cost(FLOPS),
    )(*held(*left, *cols))


def amplitudes(pair, row_term, col_term):
    low = lanes(VL)
    pieces = []
    for i in range(OCC):
        at = 128 * (i // 2)
        swapped = []
        if pair.shape[1] == 2 * OCC * VL:
            swapped = [pair[VL * j : VL * j + VL, 128 * i : 128 * i + 128] for j in range(OCC)]
        for t in range(0 if swapped else OCC // 2):
            first = pair[2 * t * VL : 2 * t * VL + VL, at : at + 128]
            second = pair[(2 * t + 1) * VL : (2 * t + 2) * VL, at : at + 128]
            if i % 2 == 0:
                second = half_turn(second)
            else:
                first = half_turn(first)
            swapped.append(jnp.where(low, first, second))
        direct = pair[VL * i : VL * i + VL, :]
        levels = row_term[VL * i : VL * i + VL, :] + col_term
        pieces.append((2.0 * direct - jnp.concatenate(swapped, axis=1)) / levels)
    return jnp.concatenate(pieces, axis=0)


def density_term(own, other, row_term, col_term, high, low):
    amplitude = amplitudes(own[...] + other[...], row_term[...], col_term[...])
    return product(split(amplitude), (high[...], low[...]), ((1,), (0,)))


def density_first_kernel(*refs):
    refs[-1][...] = density_term(*refs[:-1])


def density_next_kernel(*refs):
    refs[-1][...] = refs[-2][...] + density_term(*refs[:-2])


def density_part(inputs, before):
    args = inputs if before is None else (*inputs, before)
    return pl.pallas_call(
        density_first_kernel if before is None else density_next_kernel,
        out_shape=near_memory(PART),
        in_specs=[VMEM_SPEC] * len(args),
        out_specs=VMEM_SPEC,
        compiler_params=settings(10),
        cost_estimate=cost(FLOPS),
    )(*held(*args))


def density_last_kernel(*refs):
    before, near_0, near_1, far_0, far_1, kept_0, kept_1, whole = refs[6:]
    term = before[...] + density_term(*refs[:6])
    _, (y_a, y_b, y_far, y_own) = chip_column()
    order = (y_own, y_a, y_b, y_far)
    for q in range(QT):
        for i in range(OCC):
            for k in range(4):
                row = (i * 4 + k) * 16
                whole[q, i, order[k]] = term[row : row + 16, 128 * q : 128 * q + 128]
    low = lanes(32)
    for target, start, k in (
        (far_0, 0, 3), (far_1, 3, 3), (near_0, 0, 1), (near_1, 3, 2),
        (kept_0.at[0], 0, 0), (kept_0.at[1], 0, 2), (kept_1.at[0], 3, 0), (kept_1.at[1], 3, 1),
    ):
        y = order[k]
        for i in range(3):
            for q in range(2):
                row = (q * 3 + i) * VL
                target[row : row + VL, :] = whole[2 * y + q, start + i].reshape(VL, 128)
            rest = whole[8 + (y >> 1), start + i].reshape(VL, 128)
            rest = jnp.where((y & 1) == 1, half_turn(rest), rest)
            row = 6 * VL + 32 * i
            target[row : row + 32, :] = jnp.where(low, rest[:32], half_turn(rest[32:]))


def density_last(inputs, before):
    piece, two = near_memory((480, 128)), near_memory((2, 480, 128))
    return pl.pallas_call(
        density_last_kernel,
        out_shape=(piece,) * 4 + (two,) * 2,
        in_specs=[VMEM_SPEC] * 7,
        out_specs=(VMEM_SPEC,) * 6,
        scratch_shapes=[pltpu.VMEM((QT, OCC, 4, 16, 128), F32)],
        compiler_params=settings(12),
        cost_estimate=cost(FLOPS),
    )(*held(*inputs, before))


def unpack_kernel(kept_0, near_0, last_0, kept_1, near_1, last_1, result):
    low = lanes(VL)
    zero = chip_column()[0] == 0
    for half, refs in enumerate(((kept_0, near_0, last_0), (kept_1, near_1, last_1))):
        kept, near, last = refs
        total = kept[0] + near[...] + last[...]
        for i in range(3):
            first = total[i * VL : i * VL + VL]
            second = total[(3 + i) * VL : (4 + i) * VL]
            packed = total[6 * VL + 32 * i : 6 * VL + 32 * i + 32]
            rest = jnp.concatenate([packed, half_turn(packed)], axis=0)
            first_turned, second_turned = half_turn(first), half_turn(second)
            at = half * 3 + i
            result[at, :, 0:128] = jnp.where(zero, first, jnp.where(low, rest, first_turned))
            result[at, :, 128:256] = jnp.where(zero, second, jnp.where(low, first_turned, second_turned))
            result[at, :, 256:320] = jnp.where(zero, rest, second_turned)[:, :64]


def unpack(*parts):
    return pl.pallas_call(
        unpack_kernel,
        out_shape=jax.ShapeDtypeStruct((OCC, VL, QL), F32),
        in_specs=[VMEM_SPEC] * 6,
        out_specs=VMEM_SPEC,
        compiler_params=settings(4),
        name="unpack",
    )(*held(*parts))


def on_virt(value, pairs):
    return lax.ppermute(value, "virt", pairs)


def on_aux(value, pairs):
    return lax.ppermute(value, "aux", pairs)


SPOTS = (
    (0, 1, 0), (0, 1, 1), (0, 3, 0), (0, 3, 1), (1, 0, 0), (1, 0, 1), (3, 0, 0), (3, 0, 1),
    (0, 0, 0), (0, 0, 1), (0, 2, 0), (2, 0, 1), (1, 2, 0), (3, 2, 0), (2, 1, 1), (2, 3, 1),
    (1, 1, 0), (1, 3, 0), (3, 1, 0), (3, 3, 0), (1, 1, 1), (3, 1, 1), (1, 3, 1), (3, 3, 1),
    (2, 1, 0), (2, 3, 0), (1, 2, 1), (3, 2, 1), (2, 0, 0), (2, 2, 0), (0, 2, 1), (2, 2, 1),
)


def terms_kernel(batch_index, occ_energy, virt_energy, virt_order, row_term, *col_terms):
    place = lax.axis_index("virt").astype(jnp.int32)
    z, x = place >> 2, place & 3
    _, (y_a, y_b, y_far, y_own) = chip_column()
    chips = (y_own, y_a, y_b, y_far)
    lane = lax.broadcasted_iota(jnp.int32, (8, 128), 1).astype(F32)
    step = lax.broadcasted_iota(jnp.int32, (8, 128), 0).astype(F32)
    order = virt_order[...].astype(F32)

    def pick(table, at):
        total = jnp.zeros((8, 128), F32)
        for r in range(8):
            total = total + jnp.where(at == lane + 128.0 * r, table[r : r + 1, :], 0.0)
        return jnp.sum(total, axis=1, keepdims=True)

    spots = [(z * 4 + x, chips[r], h) for r in range(4) for h in range(2)]
    spots += [((z ^ dz) * 4 + (x ^ dx), chips[0], h) for dz, dx, h in SPOTS]
    levels = []
    for place, chip, half in spots:
        first = (place * VL + chip * 16 + half * 8).astype(F32)
        levels.append(pick(virt_energy[...], pick(order, first + step)))
    occ = [occ_energy[batch_index[i]] for i in range(OCC)]
    rows = jnp.concatenate(levels[:8], axis=0)
    for i in range(OCC):
        row_term[VL * i : VL * i + VL, :] = occ[i] - rows
    low = lax.broadcasted_iota(jnp.int32, (1, 128), 1) < 64
    for k in range(2):
        both = jnp.concatenate(levels[8 + 16 * k : 24 + 16 * k], axis=0)
        flat = jnp.broadcast_to(both, (128, 128)).T[:8]
        flat, turned = flat[:1], half_turn(flat)[:1]
        for side, value in ((0, jnp.where(low, flat, turned)), (1, jnp.where(low, turned, flat))):
            for t in range(3):
                col_terms[2 * k + side][:, 128 * t : 128 * t + 128] = jnp.where(low, occ[2 * t], occ[2 * t + 1]) - value


def energy_terms(batch_index, occ_energy, virt_energy, virt_order):
    column = near_memory((1, OCC * VL))
    return pl.pallas_call(
        terms_kernel,
        out_shape=(near_memory((OCC * VL, 1)), *(column,) * 4),
        in_specs=[SMEM_SPEC] * 2 + [VMEM_SPEC] * 2,
        out_specs=(VMEM_SPEC,) * 5,
        compiler_params=settings(4),
        cost_estimate=cost(FLOPS // 4),
        name="terms",
    )(batch_index, occ_energy, virt_energy.reshape(8, 128), virt_order.reshape(8, 128))


def shards(integrals, metric_root, occ_energy, virt_energy, batch_index, virt_order):
    values = pltpu.with_memory_space_constraint(integrals.transpose(1, 0, 2), pltpu.HBM)
    metric = pltpu.with_memory_space_constraint(metric_root.T, pltpu.HBM)

    def swap(sent, kept):
        return on_aux(sent, CORE), on_aux(kept, CORE)

    (in_sent, in_kept), (own_sent, own_kept) = fitted_parts(values, metric, swap)

    near_0, near_1, far_0, far_1 = small_call(sent_kernel, (PIECE,) * 4, (own_sent, in_sent))
    far_0, far_1 = on_aux(far_0, YA), on_aux(far_1, YB)
    near_0, near_1 = on_aux(near_0, YA), on_aux(near_1, YB)
    row_term, *col_terms = energy_terms(batch_index, occ_energy, virt_energy, virt_order)
    (last_0,) = small_call(relay_kernel(0), (PIECE,), (own_kept, in_kept, far_0))
    last_0 = on_aux(last_0, YB)
    (last_1,) = small_call(relay_kernel(1), (PIECE,), (own_kept, in_kept, far_1))
    last_1 = on_aux(last_1, YA)
    last_1, row_term, col_terms = lax.optimization_barrier((last_1, row_term, col_terms))
    parts = (own_kept, in_kept, near_0, near_1, last_0, last_1)
    (own,) = small_call(shard_kernel, ((2, *PIECE),), parts)

    s_xa, s_xb = on_virt(own, XA), on_virt(own, XB)
    s_za, s_zb = on_virt(own, ZA), on_virt(own, ZB)
    row_a, row_b = on_aux(own, YA), on_aux(own, YB)
    (beyond_a,) = small_call(pick_kernel(0), (PIECE,), (s_xa,))
    (beyond_b,) = small_call(pick_kernel(1), (PIECE,), (s_za,))
    a_2, b_2 = on_virt(beyond_a, XB), on_virt(beyond_b, ZB)
    row_2 = on_aux(own, Y2)

    (line_a,) = small_call(line_kernel(0), ((2, *PIECE),), (s_xa, s_xb))
    pa_a, pa_b = on_virt(line_a, ZA), on_virt(line_a, ZB)
    (line_b,) = small_call(line_kernel(1), ((2, *PIECE),), (s_za, s_zb))
    pb_a, pb_b = on_virt(line_b, XA), on_virt(line_b, XB)
    qa_b, qa_a = on_virt(a_2, ZB), on_virt(a_2, ZA)
    qb_b, qb_a = on_virt(b_2, XB), on_virt(b_2, XA)
    pa_2, pb_2 = on_virt(pa_a, ZB), on_virt(pb_a, XB)
    (both_a,) = small_call(join_kernel(0), ((2, *PIECE),), (s_zb, qa_b))
    (both_b,) = small_call(join_kernel(1), ((2, *PIECE),), (s_xb, qb_b))
    f_a, f_b = on_virt(both_a, ZA), on_virt(both_b, XA)

    left = rows_part(own, row_a, row_b, row_2)
    chunks = (
        (s_xa, s_xb, s_za, s_zb),
        (own, a_2, b_2, qa_a, qa_b, qb_a, qb_b),
        (pa_a, pa_b, pb_a, pb_b),
        (pa_2, pb_2, f_a, f_b),
    )
    total = None
    for k, cols in enumerate(chunks):
        pair, high, low = pair_part(left, cols)
        other = on_aux(pair, CORE)
        inputs = (pair, other, row_term, col_terms[k], high, low)
        if k < 3:
            total = density_part(inputs, total)
    near_0, near_1, far_0, far_1, kept_0, kept_1 = density_last(inputs, total)
    far_0, far_1 = on_aux(far_0, YA), on_aux(far_1, YB)
    near_0, near_1 = on_aux(near_0, YA), on_aux(near_1, YB)
    (last_0,) = small_call(final_relay_kernel, ((480, 128),), (kept_0, far_0))
    last_0 = on_aux(last_0, YB)
    (last_1,) = small_call(final_relay_kernel, ((480, 128),), (kept_1, far_1))
    last_1 = on_aux(last_1, YA)
    result = unpack(kept_0, near_0, last_0, kept_1, near_1, last_1)
    return result.transpose(1, 0, 2)


def solution(mesh):
    return jax.shard_map(
        shards,
        mesh=mesh,
        in_specs=(P("virt", None, "aux"), P(None, "aux"), P(), P(), P(), P()),
        out_specs=P("virt", None, "aux"),
        check_vma=False,
    )
```

```python
import jax
import jax.numpy as jnp
from jax import lax
from jax.experimental import pallas as pl
from jax.experimental.pallas import tpu as pltpu
from jax.sharding import PartitionSpec as P


F32 = jnp.float32
BF16 = jnp.bfloat16
OCC = 6
VL = 64
QL = 320
QH = 1280
QT = QH // 128


def plane(step_z, step_x):
    return [(z * 4 + x, (z ^ step_z) * 4 + (x ^ step_x)) for z in range(4) for x in range(4)]


def column(place, swap):
    return [(y * 2 + c, place(y) * 2 + (c ^ swap)) for y in range(4) for c in range(2)]


XA, XB = plane(0, 1), plane(0, 3)
ZA, ZB = plane(1, 0), plane(3, 0)
YA = column(lambda y: y ^ 1, 0)
YB = column(lambda y: y ^ 3, 0)
Y2 = column(lambda y: y ^ 2, 0)
CORE = column(lambda y: y, 1)


def split(value):
    high = value.astype(BF16)
    return high, (value - high.astype(F32)).astype(BF16)


def product(left, right, dims):
    left_high, left_low = left
    right_high, right_low = right

    def one(a, b):
        return lax.dot_general(a, b, (dims, ((), ())), preferred_element_type=F32)

    return one(left_high, right_low) + one(left_low, right_high) + one(left_high, right_high)


def half_turn(value):
    return pltpu.roll(value, 64, 1)


def lanes(rows):
    return lax.broadcasted_iota(jnp.int32, (rows, 128), 1) < 64


VMEM_SPEC = pl.BlockSpec(memory_space=pltpu.VMEM)
SMEM_SPEC = pl.BlockSpec(memory_space=pltpu.SMEM)
HBM_SPEC = pl.BlockSpec(memory_space=pltpu.HBM)
PIECE = (OCC, QT, 8, 128)
PART = (OCC * VL, QH)
FLOPS = 2 * 3 * (OCC * VL) ** 2 * QH


def settings(mebibytes):
    return pltpu.CompilerParams(vmem_limit_bytes=mebibytes * 2**20)


def cost(flops):
    return pl.CostEstimate(flops=flops, bytes_accessed=4 * 2**20, transcendentals=0)


def chip_column():
    place = lax.axis_index("aux").astype(jnp.int32)
    y = place >> 1
    return place & 1, (y ^ 1, y ^ 3, y ^ 2, y)


def near_memory(shape, kind=F32):
    return pltpu.VMEM(shape, kind)


def held(*values):
    return [pltpu.with_memory_space_constraint(v, pltpu.VMEM) for v in values]


def fitted_rows(left):
    rows = left[...].reshape(OCC * VL, QL)
    main_high, main_low = split(rows[:, :256])
    rest_high, rest_low = split(rows[:, 256:])
    return main_high, main_low, jnp.concatenate([rest_high, rest_low, rest_high], axis=1)


def fitted_products(core, ys, rows, right, ready, sent, kept, full):
    main_high, main_low, rest = rows
    side = pl.multiple_of(128 * core, 128)
    other = pl.multiple_of(256 - 256 * core, 128)
    low = lanes(QL)

    def put(columns, at):
        high, low_part = split(columns)
        value = product((main_high, main_low), (high[:256], low_part[:256]), ((1,), (0,)))
        ends = jnp.concatenate([low_part[256:], high[256:], high[256:]], axis=0)
        value = value + jnp.dot(rest, ends, preferred_element_type=F32)
        full[:, :, :, :, at : at + 256] = value.reshape(OCC, 4, 2, 8, 256)

    rests = []
    for y in range(4):
        ready(y)
        put(right[y, :, pl.ds(side, 256)], 256 * y)
        rests.append(right[y, :, pl.ds(other, 128)])
    packed = []
    for p in range(2):
        first, second = rests[2 * p], rests[2 * p + 1]
        even = jnp.where(low, first, half_turn(second))
        odd = jnp.where(low, half_turn(first), second)
        packed.append(jnp.where(core == 0, even, odd))
    put(jnp.concatenate(packed, axis=1), 1024)
    y_a, y_b, y_far, y_own = ys
    for target, half, slot, y in (
        (sent, 0, 0, y_a), (sent, 0, 1, y_far), (sent, 1, 0, y_b), (sent, 1, 1, y_far),
        (kept, 0, 0, y_own), (kept, 0, 1, y_b), (kept, 1, 0, y_own), (kept, 1, 1, y_a),
    ):
        for i in range(OCC):
            for q in range(QT):
                target[half, slot, i, q] = full[i, y, half, :, 128 * q : 128 * q + 128]


def partner_kernel(integrals, metric, sent, kept, left, own_right, right, full, arrivals):
    core, ys = chip_column()
    copies = [pltpu.make_async_copy(integrals, left, arrivals.at[8])]
    for k, (which, target) in enumerate(((1 - core, right), (core, own_right))):
        start = pl.multiple_of(256 * which, 128)
        for y in range(4):
            columns = metric.at[:, pl.ds(pl.multiple_of(640 * y + start, 128), 384)]
            copies.append(pltpu.make_async_copy(columns, target.at[y], arrivals.at[4 * k + y]))
    for copy in copies:
        copy.start()
    copies[0].wait()
    rows = fitted_rows(left)
    fitted_products(1 - core, ys, rows, right, lambda y: copies[1 + y].wait(), sent, kept, full)
    for copy in copies[5:]:
        copy.wait()


def self_kernel(left, right, sent, kept, full):
    core, ys = chip_column()
    fitted_products(core, ys, fitted_rows(left), right, lambda y: None, sent, kept, full)


COLUMNS = (4, QL, 384)


def fitted_parts(integrals, metric, between):
    piece = near_memory((2, 2, *PIECE))
    common = dict(compiler_params=settings(12), cost_estimate=cost(FLOPS // 3))
    sent, kept, left, right = pl.pallas_call(
        partner_kernel,
        out_shape=(piece, piece, near_memory((OCC, VL, QL)), near_memory(COLUMNS)),
        in_specs=[HBM_SPEC, HBM_SPEC],
        out_specs=(VMEM_SPEC,) * 4,
        scratch_shapes=[
            pltpu.VMEM(COLUMNS, F32),
            pltpu.VMEM((OCC, 4, 2, 8, QH), F32),
            pltpu.SemaphoreType.DMA((9,)),
        ],
        name="fitted_for_partner",
        **common,
    )(integrals, metric)
    received = between(sent, kept)
    own = pl.pallas_call(
        self_kernel,
        out_shape=(piece, piece),
        in_specs=[VMEM_SPEC] * 2,
        out_specs=(VMEM_SPEC,) * 2,
        scratch_shapes=[pltpu.VMEM((OCC, 4, 2, 8, QH), F32)],
        name="fitted_for_self",
        **common,
    )(*held(left, right))
    return received, own


def small_call(kernel, shapes, args):
    return pl.pallas_call(
        kernel,
        out_shape=tuple(near_memory(shape) for shape in shapes),
        in_specs=[VMEM_SPEC] * len(args),
        out_specs=(VMEM_SPEC,) * len(shapes),
        compiler_params=settings(4),
        cost_estimate=cost(FLOPS // 40),
    )(*held(*args))


def sent_kernel(own, other, near_0, near_1, far_0, far_1):
    for half, near, far in ((0, near_0, far_0), (1, near_1, far_1)):
        near[...] = own[half, 0] + other[half, 0]
        far[...] = own[half, 1] + other[half, 1]


def relay_kernel(half):
    def kernel(own, other, far, result):
        result[...] = own[half, 1] + other[half, 1] + far[...]

    return kernel


def shard_kernel(own, other, near_0, near_1, last_0, last_1, result):
    for half, near, last in ((0, near_0, last_0), (1, near_1, last_1)):
        result[half] = own[half, 0] + other[half, 0] + near[...] + last[...]


def line_kernel(half):
    def kernel(first, second, line):
        line[0], line[1] = first[half], second[half]

    return kernel


def join_kernel(half):
    def kernel(near, far, result):
        result[0], result[1] = near[half], far[...]

    return kernel


def pick_kernel(half):
    def kernel(value, result):
        result[...] = value[half]

    return kernel


def final_relay_kernel(kept, far, result):
    result[...] = kept[1] + far[...]


def store_split(high, low, row, q, first, second):
    value = jnp.concatenate([first, second], axis=0)
    upper, lower = split(value)
    high[row : row + 16, 128 * q : 128 * q + 128] = upper
    low[row : row + 16, 128 * q : 128 * q + 128] = lower


def rows_kernel(own, near_a, near_b, far, high, low):
    for i in range(OCC):
        for k, ref in enumerate((own, near_a, near_b, far)):
            for q in range(QT):
                store_split(high, low, (i * 4 + k) * 16, q, ref[0, i, q], ref[1, i, q])


def rows_part(*rows):
    return pl.pallas_call(
        rows_kernel,
        out_shape=(near_memory(PART, BF16),) * 2,
        in_specs=[VMEM_SPEC] * 4,
        out_specs=(VMEM_SPEC,) * 2,
        compiler_params=settings(4),
        cost_estimate=cost(FLOPS // 8),
        name="rows",
    )(*held(*rows))


def pair_kernel(left_high, left_low, *refs):
    cols = refs[:-3]
    result, high, low = refs[-3:]
    blocks = []
    for ref in cols:
        blocks += [(ref, ())] if len(ref.shape) == 4 else [(ref, (0,)), (ref, (1,))]
    count = len(blocks) // 2
    for i in range(OCC):
        for k in range(count):
            (one, at_one), (two, at_two) = blocks[2 * k], blocks[2 * k + 1]
            for q in range(QT):
                store_split(high, low, (i * count + k) * 16, q, one[(*at_one, i, q)], two[(*at_two, i, q)])
    left = left_high[...], left_low[...]
    result[...] = product(left, (high[...], low[...]), ((1,), (1,)))


def pair_part(left, cols):
    width = 48 * sum(1 if c.ndim == 4 else 2 for c in cols)
    part = near_memory((width, QH), BF16)
    return pl.pallas_call(
        pair_kernel,
        out_shape=(near_memory((OCC * VL, width)), part, part),
        in_specs=[VMEM_SPEC] * (2 + len(cols)),
        out_specs=(VMEM_SPEC,) * 3,
        compiler_params=settings(12),
        cost_estimate=cost(FLOPS),
    )(*held(*left, *cols))


def amplitudes(pair, row_term, col_term):
    low = lanes(VL)
    pieces = []
    for i in range(OCC):
        at = 128 * (i // 2)
        swapped = []
        if pair.shape[1] == 2 * OCC * VL:
            swapped = [pair[VL * j : VL * j + VL, 128 * i : 128 * i + 128] for j in range(OCC)]
        for t in range(0 if swapped else OCC // 2):
            first = pair[2 * t * VL : 2 * t * VL + VL, at : at + 128]
            second = pair[(2 * t + 1) * VL : (2 * t + 2) * VL, at : at + 128]
            if i % 2 == 0:
                second = half_turn(second)
            else:
                first = half_turn(first)
            swapped.append(jnp.where(low, first, second))
        direct = pair[VL * i : VL * i + VL, :]
        levels = row_term[VL * i : VL * i + VL, :] + col_term
        pieces.append((2.0 * direct - jnp.concatenate(swapped, axis=1)) / levels)
    return jnp.concatenate(pieces, axis=0)


def density_term(own, other, row_term, col_term, high, low):
    amplitude = amplitudes(own[...] + other[...], row_term[...], col_term[...])
    return product(split(amplitude), (high[...], low[...]), ((1,), (0,)))


def density_first_kernel(*refs):
    refs[-1][...] = density_term(*refs[:-1])


def density_next_kernel(*refs):
    refs[-1][...] = refs[-2][...] + density_term(*refs[:-2])


def density_part(inputs, before):
    args = inputs if before is None else (*inputs, before)
    return pl.pallas_call(
        density_first_kernel if before is None else density_next_kernel,
        out_shape=near_memory(PART),
        in_specs=[VMEM_SPEC] * len(args),
        out_specs=VMEM_SPEC,
        compiler_params=settings(10),
        cost_estimate=cost(FLOPS),
    )(*held(*args))


def block_columns(y):
    return pl.multiple_of(256 * y, 128), pl.multiple_of(1024 + 128 * (y >> 1), 128)


def in_row_order(value, target, order):
    for q in range(value.shape[1] // 128):
        for i in range(OCC):
            for k in range(4):
                row = (i * 4 + k) * 16
                target[q, i, order[k]] = value[row : row + 16, 128 * q : 128 * q + 128]


def put_block(target, whole, first, last, start, odd):
    low = lanes(32)
    for i in range(3):
        for q in range(2):
            row = (q * 3 + i) * VL
            target[row : row + VL, :] = whole[first + q, start + i].reshape(VL, 128)
        rest = whole[last, start + i].reshape(VL, 128)
        rest = jnp.where(odd == 1, half_turn(rest), rest)
        row = 6 * VL + 32 * i
        target[row : row + 32, :] = jnp.where(low, rest[:32], half_turn(rest[32:]))


def density_far_kernel(own, other, row_term, col_term, high, low, before, upper, lower, far_0, far_1, whole):
    _, (y_a, y_b, y_far, y_own) = chip_column()
    amplitude = split(amplitudes(own[...] + other[...], row_term[...], col_term[...]))
    upper[...], lower[...] = amplitude
    main, rest = block_columns(y_far)
    right = [jnp.concatenate([ref[:, pl.ds(main, 256)], ref[:, pl.ds(rest, 128)]], axis=1) for ref in (high, low, before)]
    in_row_order(right[2] + product(amplitude, right[:2], ((1,), (0,))), whole, (y_own, y_a, y_b, y_far))
    for target, start in ((far_0, 0), (far_1, 3)):
        put_block(target, whole, 0, 2, start, y_far & 1)


def density_rest_kernel(upper, lower, high, low, before, near_0, near_1, kept_0, kept_1, whole):
    _, (y_a, y_b, y_far, y_own) = chip_column()
    order = (y_own, y_a, y_b, y_far)
    amplitude = upper[...], lower[...]

    def columns(at):
        right = high[:, pl.ds(at, 256)], low[:, pl.ds(at, 256)]
        return before[:, pl.ds(at, 256)] + product(amplitude, right, ((1,), (0,)))

    in_row_order(columns(1024), whole.at[6:8], order)
    for k, y in enumerate((y_own, y_a, y_b)):
        in_row_order(columns(block_columns(y)[0]), whole.at[2 * k : 2 * k + 2], order)
    for target, k, y, start in (
        (near_0, 1, y_a, 0), (near_1, 2, y_b, 3),
        (kept_0.at[0], 0, y_own, 0), (kept_0.at[1], 2, y_b, 0), (kept_1.at[0], 0, y_own, 3), (kept_1.at[1], 1, y_a, 3),
    ):
        put_block(target, whole, 2 * k, 6 + (y >> 1), start, y & 1)


def density_last(inputs, before):
    piece, two = near_memory((480, 128)), near_memory((2, 480, 128))
    common = dict(compiler_params=settings(10), cost_estimate=cost(FLOPS // 2))
    square = near_memory((OCC * VL, OCC * VL), BF16)
    upper, lower, far_0, far_1 = pl.pallas_call(
        density_far_kernel,
        out_shape=(square, square, piece, piece),
        in_specs=[VMEM_SPEC] * 7,
        out_specs=(VMEM_SPEC,) * 4,
        scratch_shapes=[pltpu.VMEM((3, OCC, 4, 16, 128), F32)],
        name="density_far",
        **common,
    )(*held(*inputs, before))
    rest = pl.pallas_call(
        density_rest_kernel,
        out_shape=(piece, piece, two, two),
        in_specs=[VMEM_SPEC] * 5,
        out_specs=(VMEM_SPEC,) * 4,
        scratch_shapes=[pltpu.VMEM((8, OCC, 4, 16, 128), F32)],
        name="density_rest",
        **common,
    )(*held(upper, lower, *inputs[4:], before))
    return (far_0, far_1, *rest)


def unpack_kernel(kept_0, near_0, last_0, kept_1, near_1, last_1, result):
    low = lanes(VL)
    zero = chip_column()[0] == 0
    for half, refs in enumerate(((kept_0, near_0, last_0), (kept_1, near_1, last_1))):
        kept, near, last = refs
        total = kept[0] + near[...] + last[...]
        for i in range(3):
            first = total[i * VL : i * VL + VL]
            second = total[(3 + i) * VL : (4 + i) * VL]
            packed = total[6 * VL + 32 * i : 6 * VL + 32 * i + 32]
            rest = jnp.concatenate([packed, half_turn(packed)], axis=0)
            first_turned, second_turned = half_turn(first), half_turn(second)
            at = half * 3 + i
            result[at, :, 0:128] = jnp.where(zero, first, jnp.where(low, rest, first_turned))
            result[at, :, 128:256] = jnp.where(zero, second, jnp.where(low, first_turned, second_turned))
            result[at, :, 256:320] = jnp.where(zero, rest, second_turned)[:, :64]


def unpack(*parts):
    return pl.pallas_call(
        unpack_kernel,
        out_shape=jax.ShapeDtypeStruct((OCC, VL, QL), F32),
        in_specs=[VMEM_SPEC] * 6,
        out_specs=VMEM_SPEC,
        compiler_params=settings(4),
        name="unpack",
    )(*held(*parts))


def on_virt(value, pairs):
    return lax.ppermute(value, "virt", pairs)


def on_aux(value, pairs):
    return lax.ppermute(value, "aux", pairs)


SPOTS = (
    (0, 1, 0), (0, 1, 1), (0, 3, 0), (0, 3, 1), (1, 0, 0), (1, 0, 1), (3, 0, 0), (3, 0, 1),
    (0, 0, 0), (0, 0, 1), (0, 2, 0), (2, 0, 1), (1, 2, 0), (3, 2, 0), (2, 1, 1), (2, 3, 1),
    (1, 1, 0), (1, 3, 0), (3, 1, 0), (3, 3, 0), (1, 1, 1), (3, 1, 1), (1, 3, 1), (3, 3, 1),
    (2, 1, 0), (2, 3, 0), (1, 2, 1), (3, 2, 1), (2, 0, 0), (2, 2, 0), (0, 2, 1), (2, 2, 1),
)


def terms_kernel(batch_index, occ_energy, virt_energy, virt_order, row_term, *col_terms):
    place = lax.axis_index("virt").astype(jnp.int32)
    z, x = place >> 2, place & 3
    _, (y_a, y_b, y_far, y_own) = chip_column()
    chips = (y_own, y_a, y_b, y_far)
    lane = lax.broadcasted_iota(jnp.int32, (8, 128), 1).astype(F32)
    step = lax.broadcasted_iota(jnp.int32, (8, 128), 0).astype(F32)
    order = virt_order[...].astype(F32)

    def pick(table, at):
        total = jnp.zeros((8, 128), F32)
        for r in range(8):
            total = total + jnp.where(at == lane + 128.0 * r, table[r : r + 1, :], 0.0)
        return jnp.sum(total, axis=1, keepdims=True)

    spots = [(z * 4 + x, chips[r], h) for r in range(4) for h in range(2)]
    spots += [((z ^ dz) * 4 + (x ^ dx), chips[0], h) for dz, dx, h in SPOTS]
    levels = []
    for place, chip, half in spots:
        first = (place * VL + chip * 16 + half * 8).astype(F32)
        levels.append(pick(virt_energy[...], pick(order, first + step)))
    occ = [occ_energy[batch_index[i]] for i in range(OCC)]
    rows = jnp.concatenate(levels[:8], axis=0)
    for i in range(OCC):
        row_term[VL * i : VL * i + VL, :] = occ[i] - rows
    low = lax.broadcasted_iota(jnp.int32, (1, 128), 1) < 64
    for k in range(2):
        both = jnp.concatenate(levels[8 + 16 * k : 24 + 16 * k], axis=0)
        flat = jnp.broadcast_to(both, (128, 128)).T[:8]
        flat, turned = flat[:1], half_turn(flat)[:1]
        for side, value in ((0, jnp.where(low, flat, turned)), (1, jnp.where(low, turned, flat))):
            for t in range(3):
                col_terms[2 * k + side][:, 128 * t : 128 * t + 128] = jnp.where(low, occ[2 * t], occ[2 * t + 1]) - value


def energy_terms(batch_index, occ_energy, virt_energy, virt_order):
    column = near_memory((1, OCC * VL))
    return pl.pallas_call(
        terms_kernel,
        out_shape=(near_memory((OCC * VL, 1)), *(column,) * 4),
        in_specs=[SMEM_SPEC] * 2 + [VMEM_SPEC] * 2,
        out_specs=(VMEM_SPEC,) * 5,
        compiler_params=settings(4),
        cost_estimate=cost(FLOPS // 4),
        name="terms",
    )(batch_index, occ_energy, virt_energy.reshape(8, 128), virt_order.reshape(8, 128))


def shards(integrals, metric_root, occ_energy, virt_energy, batch_index, virt_order):
    values = pltpu.with_memory_space_constraint(integrals.transpose(1, 0, 2), pltpu.HBM)
    metric = pltpu.with_memory_space_constraint(metric_root.T, pltpu.HBM)

    def swap(sent, kept):
        return on_aux(sent, CORE), on_aux(kept, CORE)

    (in_sent, in_kept), (own_sent, own_kept) = fitted_parts(values, metric, swap)

    near_0, near_1, far_0, far_1 = small_call(sent_kernel, (PIECE,) * 4, (own_sent, in_sent))
    far_0, far_1 = on_aux(far_0, YA), on_aux(far_1, YB)
    near_0, near_1 = on_aux(near_0, YA), on_aux(near_1, YB)
    row_term, *col_terms = energy_terms(batch_index, occ_energy, virt_energy, virt_order)
    (last_0,) = small_call(relay_kernel(0), (PIECE,), (own_kept, in_kept, far_0))
    last_0 = on_aux(last_0, YB)
    (last_1,) = small_call(relay_kernel(1), (PIECE,), (own_kept, in_kept, far_1))
    last_1 = on_aux(last_1, YA)
    last_1, row_term, col_terms = lax.optimization_barrier((last_1, row_term, col_terms))
    parts = (own_kept, in_kept, near_0, near_1, last_0, last_1)
    (own,) = small_call(shard_kernel, ((2, *PIECE),), parts)

    s_xa, s_xb = on_virt(own, XA), on_virt(own, XB)
    s_za, s_zb = on_virt(own, ZA), on_virt(own, ZB)
    row_a, row_b = on_aux(own, YA), on_aux(own, YB)
    (beyond_a,) = small_call(pick_kernel(0), (PIECE,), (s_xa,))
    (beyond_b,) = small_call(pick_kernel(1), (PIECE,), (s_za,))
    a_2, b_2 = on_virt(beyond_a, XB), on_virt(beyond_b, ZB)
    row_2 = on_aux(own, Y2)

    (line_a,) = small_call(line_kernel(0), ((2, *PIECE),), (s_xa, s_xb))
    pa_a, pa_b = on_virt(line_a, ZA), on_virt(line_a, ZB)
    (line_b,) = small_call(line_kernel(1), ((2, *PIECE),), (s_za, s_zb))
    pb_a, pb_b = on_virt(line_b, XA), on_virt(line_b, XB)
    qa_b, qa_a = on_virt(a_2, ZB), on_virt(a_2, ZA)
    qb_b, qb_a = on_virt(b_2, XB), on_virt(b_2, XA)
    pa_2, pb_2 = on_virt(pa_a, ZB), on_virt(pb_a, XB)
    (both_a,) = small_call(join_kernel(0), ((2, *PIECE),), (s_zb, qa_b))
    (both_b,) = small_call(join_kernel(1), ((2, *PIECE),), (s_xb, qb_b))
    f_a, f_b = on_virt(both_a, ZA), on_virt(both_b, XA)

    left = rows_part(own, row_a, row_b, row_2)
    chunks = (
        (s_xa, s_xb, s_za, s_zb),
        (own, a_2, b_2, qa_a, qa_b, qb_a, qb_b),
        (pa_a, pa_b, pb_a, pb_b),
        (pa_2, pb_2, f_a, f_b),
    )
    total = None
    for k, cols in enumerate(chunks):
        pair, high, low = pair_part(left, cols)
        other = on_aux(pair, CORE)
        inputs = (pair, other, row_term, col_terms[k], high, low)
        if k < 3:
            total = density_part(inputs, total)
    far_0, far_1, near_0, near_1, kept_0, kept_1 = density_last(inputs, total)
    far_0, far_1 = on_aux(far_0, YA), on_aux(far_1, YB)
    near_0, near_1 = on_aux(near_0, YA), on_aux(near_1, YB)
    (last_0,) = small_call(final_relay_kernel, ((480, 128),), (kept_0, far_0))
    last_0 = on_aux(last_0, YB)
    (last_1,) = small_call(final_relay_kernel, ((480, 128),), (kept_1, far_1))
    last_1 = on_aux(last_1, YA)
    result = unpack(kept_0, near_0, last_0, kept_1, near_1, last_1)
    return result.transpose(1, 0, 2)


def solution(mesh):
    return jax.shard_map(
        shards,
        mesh=mesh,
        in_specs=(P("virt", None, "aux"), P(None, "aux"), P(), P(), P(), P()),
        out_specs=P("virt", None, "aux"),
        check_vma=False,
    )
```
